256 devices in a mesh: frame: 16 (over z_hi, x), bx: 4 (over y), by: 4 (over z_lo, core).
Axes of the slice: x: 4, y: 4, z: 8 (z_hi: 4, z_lo: 2; z = z_hi * 2 + z_lo), core: 2. Of those that a mesh axis runs over, the one named last changes fastest.
Arguments:
- features: bfloat16 [64, 16, 64, 32, 512], P('frame', None, None, 'bx', 'by'), may hold values from -26 to 26
- voxel_embed: bfloat16 [16, 64, 32, 512], P(None, None, 'bx', 'by'), may hold values from -26 to 26
- visible: int32 [64, 16, 32, 512], P('frame', None, 'bx', 'by'), may hold values from 0 to 1, as said below
- w_query: bfloat16 [64, 64], replicated, may hold values from -0.75 to 0.75
- w_key: bfloat16 [64, 64], replicated, may hold values from -0.75 to 0.75
- w_value: bfloat16 [64, 64], replicated, may hold values from -0.75 to 0.75
- w_out: bfloat16 [64, 64], replicated, may hold values from -0.75 to 0.75
- conv_weight: bfloat16 [4, 3, 3, 3, 64, 64], replicated, may hold values from -0.21875 to 0.21875
- conv_bias: float32 [4, 64], replicated, may hold values from -1.2 to 1.2
Outputs:
- volume: bfloat16 [16, 64, 32, 512], P('frame', None, 'bx', 'by')
The draws below stay inside these ranges and needn't reach their ends.
Inputs may be any that keep to these rules, and one draw needn't show every extreme that they name: Every voxel has visible = 1 in at least one of the 64 frames.
All inputs are finite; a program needn't handle non-finite values.
Results may differ from the reference program's by a relative error of at most 0.025.
Values may be sent and summed in bfloat16 or wider, within the bound.
No kernel may reach another device: no remote copies, remote signals or barrier semaphores. Data moves between devices by JAX's collectives and lax.ppermute only.
A program may use at most 64 MiB of HBM per device.

```python
import math
import jax
import jax.numpy as jnp
from jax import lax

C = 64
FR_DEV = 4
NZ = 16
LAYERS = 4
FRAMES = 64
NX = 32
NY = 512
N_FRAME = 16


def shared_surface(key):
    base = jnp.clip(jax.random.normal(jax.random.fold_in(key, 11), (NZ, C, NX, NY), jnp.float32), -4.0, 4.0)
    return base


def shared_basis(key):
    return jnp.clip(jax.random.normal(jax.random.fold_in(key, 21), (C, C), jnp.float32), -4.0, 4.0) / C ** 0.5


def draw_features(key, part):
    base = shared_surface(key)
    noise = jnp.clip(jax.random.normal(jax.random.fold_in(key, 12), (FRAMES, NZ, C, NX, NY), jnp.float32), -4.0, 4.0)
    return (base[None] + noise).astype(jnp.bfloat16)


def draw_voxel_embed(key, part):
    base = shared_surface(key)
    noise = jnp.clip(jax.random.normal(jax.random.fold_in(key, 14), (NZ, C, NX, NY), jnp.float32), -4.0, 4.0)
    level = 0.5
    return (base + level * noise).astype(jnp.bfloat16)


def draw_visible(key, part):
    coins = jax.random.randint(jax.random.fold_in(key, 31), (FRAMES, NZ, NX, NY), 0, 4)
    forced = jax.random.randint(jax.random.fold_in(key, 32), (1, NZ, NX, NY), 0, FRAMES)
    frame_ids = jnp.arange(FRAMES, dtype=jnp.int32).reshape((FRAMES, 1, 1, 1))
    return jnp.where((coins != 0) | (frame_ids == forced), 1, 0).astype(jnp.int32)


def draw_w_query(key, part):
    extra = jnp.clip(jax.random.normal(jax.random.fold_in(key, 22), (C, C), jnp.float32), -4.0, 4.0) / C ** 0.5
    return jnp.clip(shared_basis(key) + 0.5 * extra, -0.75, 0.75).astype(jnp.bfloat16)


def draw_w_key(key, part):
    extra = jnp.clip(jax.random.normal(jax.random.fold_in(key, 23), (C, C), jnp.float32), -4.0, 4.0) / C ** 0.5
    return jnp.clip(shared_basis(key) + 0.5 * extra, -0.75, 0.75).astype(jnp.bfloat16)


def bell_draw(key, shape, scale, reach, held_as=jnp.bfloat16):
    values = scale * jax.random.normal(key, shape, jnp.float32)
    return jnp.clip(values, min=-reach, max=reach).astype(held_as)


def setup_inputs(seed: int = 0) -> dict:
    keys = jax.random.split(jax.random.key(seed), 10)
    return {
        "features": draw_features(jax.random.fold_in(keys[9], 71), 0),
        "voxel_embed": draw_voxel_embed(jax.random.fold_in(keys[9], 71), 0),
        "visible": draw_visible(jax.random.fold_in(keys[9], 71), 0),
        "w_query": draw_w_query(jax.random.fold_in(keys[9], 71), 0),
        "w_key": draw_w_key(jax.random.fold_in(keys[9], 71), 0),
        "w_value": bell_draw(keys[5], (C, C), C ** -0.5, 0.75),
        "w_out": bell_draw(keys[6], (C, C), C ** -0.5, 0.75),
        "conv_weight": bell_draw(keys[7], (LAYERS, 3, 3, 3, C, C), (27 * C // 2) ** -0.5, 0.21875),
        "conv_bias": bell_draw(keys[8], (LAYERS, C), 0.3, 1.2, jnp.float32),
    }


absent_score = -1e+30
conv_layout = ('NDCHW', 'DHWIO', 'NDCHW')

def group_partial(query_data, group_feats, group_seen, w_key, w_value):
    high = lax.Precision.HIGHEST
    as_float = group_feats.astype(jnp.float32)
    key_data = jnp.einsum('fzcxy,cd->fzdxy', as_float, w_key.astype(jnp.float32), precision=high).astype(jnp.bfloat16)
    value_data = jnp.einsum('fzcxy,cd->fzdxy', as_float, w_value.astype(jnp.float32), precision=high).astype(jnp.bfloat16)
    scores = jnp.einsum('zdxy,fzdxy->fzxy', query_data.astype(jnp.float32), key_data.astype(jnp.float32), precision=high) / math.sqrt(C)
    is_seen = group_seen > 0
    highest = lax.optimization_barrier(jnp.max(jnp.where(is_seen, scores, absent_score), axis=0))
    weights = jnp.where(is_seen, jnp.exp(scores - highest[None]), 0.0)
    weighted = lax.optimization_barrier(jnp.sum(weights[:, :, None] * value_data.astype(jnp.float32), axis=0)).astype(jnp.bfloat16)
    totals = lax.optimization_barrier(jnp.sum(weights, axis=0)).astype(jnp.bfloat16)
    return (highest, weighted, totals)

def reference(features, voxel_embed, visible, w_query, w_key, w_value, w_out, conv_weight, conv_bias):
    high = lax.Precision.HIGHEST
    query_data = jnp.einsum('zcxy,cd->zdxy', voxel_embed.astype(jnp.float32), w_query.astype(jnp.float32), precision=high).astype(jnp.bfloat16)
    grouped = features.reshape((N_FRAME, FR_DEV) + features.shape[1:])
    seen_groups = visible.reshape((N_FRAME, FR_DEV) + visible.shape[1:])
    highest, weighted, totals = lax.map(lambda pair: group_partial(query_data, pair[0], pair[1], w_key, w_value), (grouped, seen_groups))
    overall = lax.optimization_barrier(jnp.max(highest, axis=0))
    factor = jnp.exp(highest - overall[None])
    merged = lax.optimization_barrier(jnp.sum(factor[:, :, None] * weighted.astype(jnp.float32), axis=0))
    norm_sum = lax.optimization_barrier(jnp.sum(factor * totals.astype(jnp.float32), axis=0))
    attended = (merged / norm_sum[:, None]).astype(jnp.bfloat16)
    hidden = jnp.einsum('zcxy,cd->zdxy', attended.astype(jnp.float32), w_out.astype(jnp.float32), precision=high).astype(jnp.bfloat16)
    for layer_no in range(LAYERS):
        result = lax.conv_general_dilated(hidden[None].astype(jnp.float32), conv_weight[layer_no].astype(jnp.float32), (1, 1, 1), ((1, 1), (1, 1), (1, 1)), dimension_numbers=conv_layout, precision=high)[0]
        result = result + conv_bias[layer_no][None, :, None, None]
        if layer_no + 1 < LAYERS:
            result = jnp.maximum(result, 0.0)
        hidden = result.astype(jnp.bfloat16)
    return hidden
```

```python
import functools

import jax
import jax.numpy as jnp
from jax import lax
from jax.experimental import pallas as pl
from jax.experimental.pallas import tpu as pltpu
from jax.sharding import PartitionSpec as P

absent_score = -1e30
halo = 4


def lane_blocks(v):
    lane = lax.broadcasted_iota(jnp.int32, (8, 128), 1)
    low = lane < 64
    even = (lane & 63) < 32
    t = [None] * 4
    for i in (0, 1):
        t[i] = jnp.where(low, v[i], pltpu.roll(v[i + 2], 64, 1))
        t[i + 2] = jnp.where(low, pltpu.roll(v[i], 64, 1), v[i + 2])
    o = [None] * 4
    for i in (0, 2):
        o[i] = jnp.where(even, t[i], pltpu.roll(t[i + 1], 32, 1))
        o[i + 1] = jnp.where(even, pltpu.roll(t[i], 96, 1), t[i + 1])
    return o


def three_terms(m):
    hi = m.astype(jnp.bfloat16).astype(jnp.float32)
    mid = (m - hi).astype(jnp.bfloat16).astype(jnp.float32)
    return hi, mid, m - hi - mid


def attend_kernel(place, feat, embed, seen, wq_t, wk, out, tmp):
    frames = feat.shape[0]
    tmp[...] = embed[0].astype(jnp.float32)
    cols = [tmp[pl.ds(i, 64, stride=8), :] for i in range(8)]
    wide = jnp.concatenate(cols, axis=1).astype(jnp.bfloat16)
    q = jnp.dot(wq_t[...], wide, preferred_element_type=jnp.float32).astype(jnp.bfloat16)
    qk = jnp.dot(wk[...], q, preferred_element_type=jnp.float32) * 0.125
    for i in range(8):
        tmp[pl.ds(i, 64, stride=8), :] = qk[:, i * 128 : (i + 1) * 128]
    sums = [jnp.zeros((8, 128), jnp.float32) for _ in range(frames)]
    for g in range(16):
        rows = slice(32 * g, 32 * g + 32)
        key = tmp[rows, :]
        for f in range(frames):
            prod = (key * feat[f, 0, rows, :].astype(jnp.float32)).reshape(4, 8, 128)
            sums[f] = sums[f] + jnp.sum(prod, axis=0)
    ok = [seen[f, 0] > 0 for f in range(frames)]
    m = jnp.full((8, 128), absent_score, jnp.float32)
    for f in range(frames):
        m = jnp.maximum(m, jnp.where(ok[f], sums[f], absent_score))
    e = [jnp.where(ok[f], jnp.exp(sums[f] - m), 0.0) for f in range(frames)]
    total = e[0]
    for f in range(1, frames):
        total = total + e[f]
    mine = place[0]

    def put(g, tiles):
        for k, tile in enumerate(lane_blocks(tiles)):
            slot = (k - mine) & 3
            out[slot, 0, 8 * g : 8 * g + 8, :] = tile.astype(jnp.bfloat16)

    for g in range(16):
        rows = slice(32 * g, 32 * g + 32)
        acc = jnp.zeros((4, 8, 128), jnp.float32)
        for f in range(frames):
            acc = acc + e[f][None] * feat[f, 0, rows, :].astype(jnp.float32).reshape(4, 8, 128)
        put(g, [acc[i] for i in range(4)])
    put(16, [*three_terms(m), total])


def attend(place, features, voxel_embed, visible, w_query, w_key):
    frames, planes, c = features.shape[:3]
    feat = features.reshape(frames, planes, c * 8, 128)
    embed = voxel_embed.reshape(planes, c * 8, 128)

    def out_map(z, place):
        return (0, ((z // 4 - place[1]) & 3) * 4 + z % 4, 0, 0)

    return pl.pallas_call(
        attend_kernel,
        out_shape=jax.ShapeDtypeStruct((4, planes, 136, 128), jnp.bfloat16),
        grid_spec=pltpu.PrefetchScalarGridSpec(
            num_scalar_prefetch=1,
            grid=(planes,),
            in_specs=[
                pl.BlockSpec((frames, 1, c * 8, 128), lambda z, p: (0, z, 0, 0)),
                pl.BlockSpec((1, c * 8, 128), lambda z, p: (z, 0, 0)),
                pl.BlockSpec((frames, 1, 8, 128), lambda z, p: (0, z, 0, 0)),
                pl.BlockSpec((c, c), lambda z, p: (0, 0)),
                pl.BlockSpec((c, c), lambda z, p: (0, 0)),
            ],
            out_specs=pl.BlockSpec((4, 1, 136, 128), out_map),
            scratch_shapes=[pltpu.VMEM((c * 8, 128), jnp.float32)],
        ),
        compiler_params=pltpu.CompilerParams(dimension_semantics=("arbitrary",)),
        name="attend",
    )(place, feat, embed, visible, w_query.T, w_key)


def spread(v):
    u = v + pltpu.roll(v, 64, 1)
    return u + pltpu.roll(u, 32, 1)


def merge_kernel(last, *refs):
    parts, out = refs[:-1], refs[-1]
    lane = lax.broadcasted_iota(jnp.int32, (8, 128), 1)
    tail = lane >= 96
    for p in range(out.shape[0]):
        stats = [r[p, 128:136, :].astype(jnp.float32) for r in parts]
        ms = [spread(jnp.where(tail, 0.0, s)) for s in stats]
        ls = [spread(jnp.where(tail, s, 0.0)) for s in stats]
        m = functools.reduce(jnp.maximum, ms)
        ws = [jnp.exp(v - m) for v in ms]
        total = sum(w * v for w, v in zip(ws, ls))
        if last:
            inv = 1.0 / total
            ws = [w * inv for w in ws]
        acc = None
        for r, w in zip(parts, ws):
            term = r[p, 0:128, :].astype(jnp.float32).reshape(16, 8, 128) * w[None]
            acc = term if acc is None else acc + term
        out[p, 0:128, :] = acc.reshape(128, 128).astype(jnp.bfloat16)
        if not last:
            hi, mid, low = three_terms(m)
            packed = jnp.where(
                lane < 32, hi, jnp.where(lane < 64, mid, jnp.where(tail, total, low))
            )
            out[p, 128:136, :] = packed.astype(jnp.bfloat16)


def merge(parts, last=False):
    n = parts[0].shape[0]
    step = min(n, 2)
    spec = pl.BlockSpec((step, 136, 128), lambda i: (i, 0, 0))
    rows = 128 if last else 136
    return pl.pallas_call(
        functools.partial(merge_kernel, last),
        out_shape=jax.ShapeDtypeStruct((n, rows, 128), jnp.bfloat16),
        grid=(n // step,),
        in_specs=[spec] * len(parts),
        out_specs=pl.BlockSpec((step, rows, 128), lambda i: (i, 0, 0)),
        name="merge",
    )(*parts)


def ring_reduce(slots, up, down, last=False):
    half = slots[0].shape[0] // 2
    from_low = lax.ppermute(slots[2][:half], "frame", up)
    from_high = lax.ppermute(slots[2][half:], "frame", down)
    first = jnp.concatenate([merge([slots[1][:half], from_low]), slots[1][half:]])
    third = jnp.concatenate([slots[3][:half], merge([slots[3][half:], from_high])])
    from_low = lax.ppermute(first, "frame", up)
    from_high = lax.ppermute(third, "frame", down)
    return merge([slots[0], from_low, from_high], last)


def banded(w):
    c, o = w.shape[-2:]
    blocks = jnp.zeros((3, 3, 6, c, 4, o), w.dtype)
    for j in range(4):
        for a in range(3):
            blocks = blocks.at[:, :, j + a, :, j, :].set(w[a])
    return blocks.reshape(3, 3, 6 * c, 4 * o)


def shards(features, voxel_embed, visible, w_query, w_key, w_value, w_out, conv_weight, conv_bias):
    me = lax.axis_index("frame")
    zh, xi = me // 4, me % 4
    place = jnp.stack([xi, zh]).astype(jnp.int32)
    x_up = [(4 * z + x, 4 * z + (x + 1) % 4) for z in range(4) for x in range(4)]
    x_down = [(j, i) for i, j in x_up]
    z_up = [(4 * z + x, 4 * ((z + 1) % 4) + x) for z in range(4) for x in range(4)]
    z_down = [(j, i) for i, j in z_up]
    slots = attend(place, features, voxel_embed, visible, w_query, w_key)
    mixed = ring_reduce([slots[r] for r in range(4)], x_up, x_down)
    mixed = ring_reduce([mixed[4 * r : 4 * r + 4] for r in range(4)], z_up, z_down, True)
    mixed = mixed.reshape(4, 16, 8, 4, 32).transpose(2, 4, 0, 1, 3).reshape(8, 32, 4, 64)
    attended = jnp.einsum(
        "xyzc,cd->xyzd", mixed, w_value, preferred_element_type=jnp.float32
    ).astype(jnp.bfloat16)
    hidden = jnp.einsum(
        "xyzc,cd->xyzd", attended, w_out, preferred_element_type=jnp.float32
    ).astype(jnp.bfloat16).reshape(8, 32, 256)

    z_next = [(i, i + 4) for i in range(12)]
    z_prev = [(j, i) for i, j in z_next]
    below = lax.ppermute(hidden, "frame", z_next)
    above = lax.ppermute(hidden, "frame", z_prev)
    hidden = jnp.concatenate([below, hidden, above], axis=2)

    def where_is(z, chunk):
        return (4 * z + chunk % 4) * 4 + chunk // 4

    y_next = [(where_is(z, k), where_is(z, k + 1)) for z in range(4) for k in range(15)]
    y_prev = [(j, i) for i, j in y_next]
    left = lax.ppermute(hidden[:, -halo:], ("frame", "by"), y_next)
    right = lax.ppermute(hidden[:, :halo], ("frame", "by"), y_prev)
    hidden = jnp.concatenate([left, hidden, right], axis=1)
    x_next = [(0, 1), (1, 2), (2, 3)]
    x_prev = [(j, i) for i, j in x_next]
    front = lax.ppermute(hidden[-halo:], "bx", x_next)
    back = lax.ppermute(hidden[:halo], "bx", x_prev)
    hidden = jnp.concatenate([front, hidden, back], axis=0)

    x0 = lax.axis_index("bx") * 8
    y0 = lax.axis_index("by") * 128 + xi * 32
    z0 = zh * 4
    layers = conv_weight.shape[0]
    for layer in range(layers):
        w = banded(conv_weight[layer])
        width = halo - 1 - layer
        planes = 4 + 2 * width
        pieces = []
        for start in range(0, planes, 4):
            count = min(4, planes - start)
            part = hidden[:, :, start * 64 : (start + count + 2) * 64]
            pieces.append(
                lax.conv_general_dilated(
                    part[None],
                    w[:, :, : (count + 2) * 64, : count * 64],
                    (1, 1),
                    "VALID",
                    dimension_numbers=("NHWC", "HWIO", "NHWC"),
                    preferred_element_type=jnp.float32,
                )[0]
            )
        h = jnp.concatenate(pieces, axis=2) + jnp.tile(conv_bias[layer], planes)
        if layer + 1 < layers:
            h = jnp.maximum(h, 0.0)
            xs = x0 - width + jnp.arange(h.shape[0])
            ys = y0 - width + jnp.arange(h.shape[1])
            zs = z0 - width + jnp.arange(planes * 64) // 64
            inside = (
                ((xs >= 0) & (xs < 32))[:, None, None]
                & ((ys >= 0) & (ys < 512))[None, :, None]
                & ((zs >= 0) & (zs < 16))[None, None, :]
            )
            h = jnp.where(inside, h, 0.0)
        hidden = h.astype(jnp.bfloat16)
    groups = [[4 * z + x for x in range(4)] for z in range(4)]
    out = hidden.reshape(256, 256).T.reshape(4, 64, 256)
    out = lax.all_to_all(out, "frame", 0, 0, axis_index_groups=groups, tiled=True)
    out = out.reshape(4, 64, 8, 32).transpose(1, 2, 0, 3).reshape(1, 64, 8, 128)
    return out


def solution(mesh):
    return jax.shard_map(
        shards,
        mesh=mesh,
        in_specs=(
            P("frame", None, None, "bx", "by"),
            P(None, None, "bx", "by"),
            P("frame", None, "bx", "by"),
            P(),
            P(),
            P(),
            P(),
            P(),
            P(),
        ),
        out_specs=P("frame", None, "bx", "by"),
        check_vma=False,
    )
```

```python
import functools

import jax
import jax.numpy as jnp
from jax import lax
from jax.experimental import pallas as pl
from jax.experimental.pallas import tpu as pltpu
from jax.sharding import PartitionSpec as P

absent_score = -1e30
halo = 4
stride = 48
bf16, f32 = jnp.bfloat16, jnp.float32
VM = pl.BlockSpec(memory_space=pltpu.VMEM)


def dot(a, b):
    return jnp.dot(a, b, preferred_element_type=f32)


def lane_blocks(v):
    lane = lax.broadcasted_iota(jnp.int32, (8, 128), 1)
    low = lane < 64
    even = (lane & 63) < 32
    t = [None] * 4
    for i in (0, 1):
        t[i] = jnp.where(low, v[i], pltpu.roll(v[i + 2], 64, 1))
        t[i + 2] = jnp.where(low, pltpu.roll(v[i], 64, 1), v[i + 2])
    o = [None] * 4
    for i in (0, 2):
        o[i] = jnp.where(even, t[i], pltpu.roll(t[i + 1], 32, 1))
        o[i + 1] = jnp.where(even, pltpu.roll(t[i], 96, 1), t[i + 1])
    return o


def three_terms(m):
    hi = m.astype(bf16).astype(f32)
    mid = (m - hi).astype(bf16).astype(f32)
    return hi, mid, m - hi - mid


def attend_kernel(place, feat, embed, seen, wq, wk, *refs):
    outs, tmp = refs[:4], refs[4]
    frames, planes = feat.shape[:2]
    turn = (128 - 32 * place[0]) & 127
    for p in range(planes):
        tmp[p] = embed[p].astype(f32)
    cols = [tmp[p, pl.ds(i, 64, stride=8), :] for p in range(planes) for i in range(8)]
    wide = jnp.concatenate(cols, axis=1).astype(bf16)
    q = lax.dot_general(wq[...], wide, (((0,), (0,)), ((), ())), preferred_element_type=f32)
    qk = dot(wk[...], q.astype(bf16)) * 0.125
    for p in range(planes):
        for i in range(8):
            at = (8 * p + i) * 128
            tmp[p, pl.ds(i, 64, stride=8), :] = qk[:, at : at + 128]
    for p in range(planes):
        sums = [jnp.zeros((8, 128), f32) for _ in range(frames)]
        for g in range(16):
            rows = slice(32 * g, 32 * g + 32)
            key = tmp[p, rows, :]
            for f in range(frames):
                prod = (key * feat[f, p, rows, :].astype(f32)).reshape(4, 8, 128)
                sums[f] = sums[f] + jnp.sum(prod, axis=0)
        ok = [seen[f, p] > 0 for f in range(frames)]
        m = jnp.full((8, 128), absent_score, f32)
        for f in range(frames):
            m = jnp.maximum(m, jnp.where(ok[f], sums[f], absent_score))
        e = [jnp.where(ok[f], jnp.exp(sums[f] - m), 0.0) for f in range(frames)]
        total = e[0]
        for f in range(1, frames):
            total = total + e[f]

        def put(g, tiles):
            tiles = [pltpu.roll(t, turn, 1) for t in tiles]
            for out, tile in zip(outs, lane_blocks(tiles)):
                out[p, 8 * g : 8 * g + 8, :] = tile.astype(bf16)

        for g in range(16):
            rows = slice(32 * g, 32 * g + 32)
            acc = jnp.zeros((4, 8, 128), f32)
            for f in range(frames):
                acc = acc + e[f][None] * feat[f, p, rows, :].astype(f32).reshape(4, 8, 128)
            put(g, [acc[i] for i in range(4)])
        put(16, [*three_terms(m), total])


def attend(half, place, feat, embed, visible, w_query, w_key):
    frames, planes, rows = feat.shape[:3]
    c = w_key.shape[0]
    n = 2
    count = planes // 2

    def block(i, place):
        rel = half * count + i * n
        return (((rel // 4 + place[1]) & 3) * 4 + rel % 4) // n

    return pl.pallas_call(
        attend_kernel,
        out_shape=[jax.ShapeDtypeStruct((count, 136, 128), bf16)] * 4,
        grid_spec=pltpu.PrefetchScalarGridSpec(
            num_scalar_prefetch=1,
            grid=(count // n,),
            in_specs=[
                pl.BlockSpec((frames, n, rows, 128), lambda i, p: (0, block(i, p), 0, 0)),
                pl.BlockSpec((n, rows, 128), lambda i, p: (block(i, p), 0, 0)),
                pl.BlockSpec((frames, n, 8, 128), lambda i, p: (0, block(i, p), 0, 0)),
                pl.BlockSpec((c, c), lambda i, p: (0, 0)),
                pl.BlockSpec((c, c), lambda i, p: (0, 0)),
            ],
            out_specs=[pl.BlockSpec((n, 136, 128), lambda i, p: (i, 0, 0))] * 4,
            scratch_shapes=[pltpu.VMEM((n, rows, 128), f32)],
        ),
        compiler_params=pltpu.CompilerParams(
            dimension_semantics=("arbitrary",), vmem_limit_bytes=12 << 20
        ),
        cost_estimate=pl.CostEstimate(flops=10**8, bytes_accessed=12 << 20, transcendentals=0),
        name="attend",
    )(place, feat, embed, visible, w_query, w_key)


def spread(v):
    u = v + pltpu.roll(v, 64, 1)
    return u + pltpu.roll(u, 32, 1)


def merged_plane(parts):
    lane = lax.broadcasted_iota(jnp.int32, (8, 128), 1)
    tail = lane >= 96
    stats = [r[p, 128:136, :].astype(f32) for r, p in parts]
    ms = [spread(jnp.where(tail, 0.0, s)) for s in stats]
    ls = [spread(jnp.where(tail, s, 0.0)) for s in stats]
    m = functools.reduce(jnp.maximum, ms)
    ws = [jnp.exp(v - m) for v in ms]
    total = sum(w * v for w, v in zip(ws, ls))
    return ws, total, m


def weighted_rows(parts, ws):
    acc = None
    for (r, p), w in zip(parts, ws):
        term = r[p, 0:128, :].astype(f32).reshape(16, 8, 128) * w[None]
        acc = term if acc is None else acc + term
    return acc.reshape(128, 128)


def merge_kernel(n, sizes, *refs):
    ins, outs = refs[:n], refs[n:]
    lane = lax.broadcasted_iota(jnp.int32, (8, 128), 1)
    at = 0
    for out, size in zip(outs, sizes):
        for i in range(size):
            parts = [(r, at) for r in ins]
            ws, total, m = merged_plane(parts)
            out[i, 0:128, :] = weighted_rows(parts, ws).astype(bf16)
            hi, mid, low = three_terms(m)
            packed = jnp.where(
                lane < 32, hi, jnp.where(lane < 64, mid, jnp.where(lane >= 96, total, low))
            )
            out[i, 128:136, :] = packed.astype(bf16)
            at += 1


def merge(parts, sizes):
    n = parts[0].shape[0]
    return pl.pallas_call(
        functools.partial(merge_kernel, len(parts), sizes),
        out_shape=[jax.ShapeDtypeStruct((s, 136, 128), bf16) for s in sizes],
        in_specs=[VM] * len(parts),
        out_specs=[VM] * len(sizes),
        compiler_params=pltpu.CompilerParams(vmem_limit_bytes=6 << 20),
        cost_estimate=pl.CostEstimate(flops=n * 10**5, bytes_accessed=n * 10**5, transcendentals=0),
        name="merge",
    )(*parts)


def finish_kernel(own, low_a, low_b, high_a, high_b, wv, wo, out, rows):
    for p in range(4):
        low, high = (low_a, high_a) if p < 2 else (low_b, high_b)
        parts = [(own, p), (low, p % 2), (high, p % 2)]
        ws, total, _ = merged_plane(parts)
        inv = 1.0 / total
        rows[128 * p : 128 * p + 128, :] = weighted_rows(parts, [w * inv for w in ws])
    lines = []
    for x in range(8):
        t = rows[pl.ds(x, 64, stride=8), :].T
        lines.append(jnp.concatenate([t[32 * i : 32 * i + 32] for i in range(4)], axis=1))
    mixed = jnp.concatenate(lines, axis=0).astype(bf16)
    attended = dot(mixed, wv[...]).astype(bf16)
    out[...] = dot(attended, wo[...]).astype(bf16)


def finish(own, low_a, low_b, high_a, high_b, wv, wo):
    return pl.pallas_call(
        finish_kernel,
        out_shape=jax.ShapeDtypeStruct((256, 256), bf16),
        in_specs=[VM] * 7,
        out_specs=VM,
        scratch_shapes=[pltpu.VMEM((512, 128), f32)],
        compiler_params=pltpu.CompilerParams(vmem_limit_bytes=6 << 20),
        name="finish",
    )(own, low_a, low_b, high_a, high_b, wv, wo)


def weights_kernel(w, wv, wo, band, wide_v, wide_o, tmp):
    zero = jnp.zeros((64, 64), bf16)
    for tap in range(9):
        a = [w[0, 9 * i + tap] for i in range(3)]
        left = jnp.concatenate([a[0], a[1], a[2], zero], axis=0)
        right = jnp.concatenate([zero, a[0], a[1], a[2]], axis=0)
        band[0, tap] = jnp.concatenate([left, right], axis=1)

    @pl.when(pl.program_id(0) == 0)
    def _():
        tmp[...] = wv[...].astype(f32)
        blank = jnp.zeros((16, 64), f32)
        for i in range(4):
            piece = tmp[pl.ds(i, 16, stride=4), :]
            for p in range(4):
                line = jnp.concatenate([piece if j == p else blank for j in range(4)], axis=1)
                at = 64 * i + 16 * p
                wide_v[at : at + 16, :] = line.astype(bf16)
        for p in range(4):
            line = jnp.concatenate([wo[...] if j == p else zero for j in range(4)], axis=1)
            wide_o[64 * p : 64 * p + 64, :] = line


def weights(conv_weight, w_value, w_out):
    layers = conv_weight.shape[0]
    small = pl.BlockSpec((64, 64), lambda i: (0, 0))
    big = pl.BlockSpec((256, 256), lambda i: (0, 0))
    return pl.pallas_call(
        weights_kernel,
        out_shape=[
            jax.ShapeDtypeStruct((layers, 9, 256, 128), bf16),
            jax.ShapeDtypeStruct((256, 256), bf16),
            jax.ShapeDtypeStruct((256, 256), bf16),
        ],
        grid=(layers,),
        in_specs=[pl.BlockSpec((1, 27, 64, 64), lambda i: (i, 0, 0, 0)), small, small],
        out_specs=[pl.BlockSpec((1, 9, 256, 128), lambda i: (i, 0, 0, 0)), big, big],
        scratch_shapes=[pltpu.VMEM((64, 64), f32)],
        compiler_params=pltpu.CompilerParams(
            dimension_semantics=("arbitrary",), vmem_limit_bytes=8 << 20
        ),
        cost_estimate=pl.CostEstimate(flops=10**6, bytes_accessed=8 << 20, transcendentals=0),
        name="weights",
    )(conv_weight.reshape(layers, 27, 64, 64), w_value, w_out)


def conv_kernel(where, block, band, bias, out, buf0, buf1, mask):
    layers = band.shape[0]
    x0, y0, z0 = where[0], where[1], where[2]
    y = lax.broadcasted_iota(jnp.int32, (stride, 128), 0) + (y0 - halo)
    y_ok = (y >= 0) & (y < 512)
    for x in range(16):
        x_at = x0 - halo + x
        line = jnp.where(y_ok & (x_at >= 0) & (x_at < 32), 1.0, 0.0)
        mask[stride * x : stride * x + stride, :] = line
    lane = lax.broadcasted_iota(jnp.int32, (1, 128), 1)

    def spread_rows(buf, value, at, lanes):
        n = value.shape[0]
        buf[1, at : at + n, lanes] = value.astype(bf16)
        buf[0, at : at + n, lanes] = pltpu.roll(value, 1, 0).astype(bf16)
        buf[2, at : at + n, lanes] = pltpu.roll(value, n - 1, 0).astype(bf16)

    for i in range(6):
        lanes = slice(128 * i, 128 * i + 128)
        spread_rows(buf0, block[:, lanes].astype(f32), 0, lanes)
    src, dst = buf0, buf1
    for layer in range(layers):
        first = stride * (layer + 1)
        n = stride * (14 - 2 * layer)
        last = layer + 1 == layers

        def pair(t, carry, src=src, dst=dst, layer=layer, first=first, n=n, last=last):
            lanes_in = pl.ds(pl.multiple_of(128 * t, 128), 256)
            lanes_out = pl.ds(pl.multiple_of(128 * t, 128), 128)
            acc = jnp.zeros((n, 128), f32)
            for b in range(3):
                rows = slice(first + stride * (b - 1), first + stride * (b - 1) + n)
                for e in range(3):
                    acc = acc + dot(src[e, rows, lanes_in], band[layer, 3 * b + e])
            acc = acc + bias[layer : layer + 1, :]
            if last:
                acc = pltpu.roll(acc, n - halo, 0)
                tiles = [acc[stride * x : stride * x + 32] for x in range(8)]
                whole = jnp.concatenate(tiles, axis=0).T
                out[pl.ds(pl.multiple_of(128 * t, 128), 128), :] = whole.astype(bf16)
            else:
                z = z0 - halo + layer + 1 + 2 * t + lane // 64
                ok = jnp.where((z >= 0) & (z < 16), 1.0, 0.0) * mask[first : first + n, :]
                spread_rows(dst, jnp.where(ok > 0, jnp.maximum(acc, 0.0), 0.0), first, lanes_out)
            return carry

        lax.fori_loop(0, 5 - layer, pair, 0)
        src, dst = dst, src


def convolve(where, block, band, bias):
    return pl.pallas_call(
        conv_kernel,
        out_shape=jax.ShapeDtypeStruct((256, 256), bf16),
        in_specs=[pl.BlockSpec(memory_space=pltpu.SMEM), VM, VM, VM],
        out_specs=VM,
        scratch_shapes=[
            pltpu.VMEM((3, 16 * stride, 768), bf16),
            pltpu.VMEM((3, 16 * stride, 640), bf16),
            pltpu.VMEM((16 * stride, 128), f32),
        ],
        compiler_params=pltpu.CompilerParams(vmem_limit_bytes=24 << 20),
        name="convolve",
    )(where, block, band, bias)


def ring_step(s1a, s1b, s2a, s2b, s3a, s3b, up, down):
    send = lambda v, way: lax.ppermute(v, "frame", way)
    from_low, from_high = send(s2a, up), send(s2b, down)
    low_b, high_a = send(s1b, up), send(s3a, down)
    n = s1a.shape[0]
    low_a = send(merge([s1a, from_low], [n])[0], up)
    high_b = send(merge([s3b, from_high], [n])[0], down)
    return low_a, low_b, high_a, high_b


def shards(features, voxel_embed, visible, w_query, w_key, w_value, w_out, conv_weight, conv_bias):
    me = lax.axis_index("frame")
    zh, xi = me // 4, me % 4
    place = jnp.stack([xi, zh]).astype(jnp.int32)
    x_up = [(4 * z + x, 4 * z + (x + 1) % 4) for z in range(4) for x in range(4)]
    x_down = [(j, i) for i, j in x_up]
    z_up = [(4 * z + x, 4 * ((z + 1) % 4) + x) for z in range(4) for x in range(4)]
    z_down = [(j, i) for i, j in z_up]
    frames, planes, c = features.shape[:3]
    feat = features.reshape(frames, planes, c * 8, 128)
    embed = voxel_embed.reshape(planes, c * 8, 128)
    a0, a1, a2, a3 = attend(0, place, feat, embed, visible, w_query, w_key)
    b0, b1, b2, b3 = attend(1, place, feat, embed, visible, w_query, w_key)
    band, wide_v, wide_o = weights(conv_weight, w_value, w_out)
    low_a, low_b, high_a, high_b = ring_step(a1, b1, a2, b2, a3, b3, x_up, x_down)
    z2a, z2b, z3a, z3b = merge([b0, low_b, high_b], [2, 2, 2, 2])
    z0, z1a, z1b = merge([a0, low_a, high_a], [4, 2, 2])
    rest = ring_step(z1a, z1b, z2a, z2b, z3a, z3b, z_up, z_down)
    hidden = finish(z0, *rest, wide_v, wide_o).reshape(8, 32, 256)

    z_next = [(i, i + 4) for i in range(12)]
    z_prev = [(j, i) for i, j in z_next]
    below = lax.ppermute(hidden, "frame", z_next)
    above = lax.ppermute(hidden, "frame", z_prev)
    hidden = jnp.concatenate([below, hidden, above], axis=2)

    def where_is(z, chunk):
        return (4 * z + chunk % 4) * 4 + chunk // 4

    y_next = [(where_is(z, k), where_is(z, k + 1)) for z in range(4) for k in range(15)]
    y_prev = [(j, i) for i, j in y_next]
    left = lax.ppermute(hidden[:, -halo:], ("frame", "by"), y_next)
    right = lax.ppermute(hidden[:, :halo], ("frame", "by"), y_prev)
    pad = jnp.zeros((8, stride - 32 - 2 * halo, 768), bf16)
    hidden = jnp.concatenate([left, hidden, right, pad], axis=1)
    x_next = [(0, 1), (1, 2), (2, 3)]
    x_prev = [(j, i) for i, j in x_next]
    front = lax.ppermute(hidden[-halo:], "bx", x_next)
    back = lax.ppermute(hidden[:halo], "bx", x_prev)
    hidden = jnp.concatenate([front, hidden, back], axis=0)

    where = jnp.stack(
        [lax.axis_index("bx") * 8, lax.axis_index("by") * 128 + xi * 32, zh * 4]
    ).astype(jnp.int32)
    bias = jnp.concatenate([conv_bias, conv_bias], axis=1)
    out = convolve(where, hidden.reshape(16 * stride, 768), band, bias)
    groups = [[4 * z + x for x in range(4)] for z in range(4)]
    out = lax.all_to_all(
        out.reshape(4, 64, 256), "frame", 0, 0, axis_index_groups=groups, tiled=True
    )
    return out.reshape(4, 64, 8, 32).transpose(1, 2, 0, 3).reshape(1, 64, 8, 128)


def solution(mesh):
    return jax.shard_map(
        shards,
        mesh=mesh,
        in_specs=(
            P("frame", None, None, "bx", "by"),
            P(None, None, "bx", "by"),
            P("frame", None, "bx", "by"),
            P(),
            P(),
            P(),
            P(),
            P(),
            P(),
        ),
        out_specs=P("frame", None, "bx", "by"),
        check_vma=False,
    )
```

```python
import functools

import jax
import jax.numpy as jnp
from jax import lax
from jax.experimental import pallas as pl
from jax.experimental.pallas import tpu as pltpu
from jax.sharding import PartitionSpec as P


absent_score = -1e30
halo = 4
stride = 48
bf16, f32 = jnp.bfloat16, jnp.float32
VM = pl.BlockSpec(memory_space=pltpu.VMEM)


def dot(a, b):
    return jnp.dot(a, b, preferred_element_type=f32)


def lane_blocks(v):
    lane = lax.broadcasted_iota(jnp.int32, (8, 128), 1)
    low = lane < 64
    even = (lane & 63) < 32
    t = [None] * 4
    for i in (0, 1):
        t[i] = jnp.where(low, v[i], pltpu.roll(v[i + 2], 64, 1))
        t[i + 2] = jnp.where(low, pltpu.roll(v[i], 64, 1), v[i + 2])
    o = [None] * 4
    for i in (0, 2):
        o[i] = jnp.where(even, t[i], pltpu.roll(t[i + 1], 32, 1))
        o[i + 1] = jnp.where(even, pltpu.roll(t[i], 96, 1), t[i + 1])
    return o


def three_terms(m):
    hi = m.astype(bf16).astype(f32)
    mid = (m - hi).astype(bf16).astype(f32)
    return hi, mid, m - hi - mid


def attend_kernel(half, feat_at, embed_at, seen_at, wq_at, wk_at, *refs):
    outs, feat, embed, seen, wq, wk, key0, key1, sems = refs[:4], *refs[4:]
    steps, frames, n = feat.shape[:3]
    me = lax.axis_index("frame")
    zh, xi = me // 4, me % 4
    turn = (128 - 32 * xi) & 127

    def copies(s):
        rel = half * steps * n + s * n
        z = pl.ds(((rel // 4 + zh) & 3) * 4 + rel % 4, n)
        return [
            pltpu.make_async_copy(embed_at.at[z], embed.at[s], sems.at[s, 0]),
            pltpu.make_async_copy(feat_at.at[:, z], feat.at[s], sems.at[s, 1]),
            pltpu.make_async_copy(seen_at.at[:, z], seen.at[s], sems.at[s, 2]),
        ]

    loads = [copies(s) for s in range(steps)]
    small = [
        pltpu.make_async_copy(wq_at, wq, sems.at[steps, 0]),
        pltpu.make_async_copy(wk_at, wk, sems.at[steps, 1]),
    ]
    for c in [loads[0][0], *small, *loads[0][1:], *sum(loads[1:], [])]:
        c.start()
    for c in small:
        c.wait()

    def keys(s):
        key = (key0, key1)[s % 2]
        loads[s][0].wait()
        for p in range(n):
            key[p] = embed[s, p].astype(f32)
        cols = [key[p, pl.ds(i, 64, stride=8), :] for p in range(n) for i in range(8)]
        wide = jnp.concatenate(cols, axis=1).astype(bf16)
        q = lax.dot_general(wq[...], wide, (((0,), (0,)), ((), ())), preferred_element_type=f32)
        qk = dot(wk[...], q.astype(bf16)) * 0.125
        for p in range(n):
            for i in range(8):
                at = (8 * p + i) * 128
                key[p, pl.ds(i, 64, stride=8), :] = qk[:, at : at + 128]

    def plane(s, p):
        key = (key0, key1)[s % 2]
        sums = [jnp.zeros((8, 128), f32) for _ in range(frames)]
        for g in range(16):
            rows = slice(32 * g, 32 * g + 32)
            line = key[p, rows, :]
            for f in range(frames):
                prod = (line * feat[s, f, p, rows, :].astype(f32)).reshape(4, 8, 128)
                sums[f] = sums[f] + jnp.sum(prod, axis=0)
        ok = [seen[s, f, p] > 0 for f in range(frames)]
        m = jnp.full((8, 128), absent_score, f32)
        for f in range(frames):
            m = jnp.maximum(m, jnp.where(ok[f], sums[f], absent_score))
        e = [jnp.where(ok[f], jnp.exp(sums[f] - m), 0.0) for f in range(frames)]
        total = e[0]
        for f in range(1, frames):
            total = total + e[f]

        def put(g, tiles):
            tiles = [pltpu.roll(t, turn, 1) for t in tiles]
            for out, tile in zip(outs, lane_blocks(tiles)):
                out[s * n + p, 8 * g : 8 * g + 8, :] = tile.astype(bf16)

        for g in range(16):
            rows = slice(32 * g, 32 * g + 32)
            acc = None
            for f in range(frames):
                term = e[f][None] * feat[s, f, p, rows, :].astype(f32).reshape(4, 8, 128)
                acc = term if acc is None else acc + term
            put(g, [acc[i] for i in range(4)])
        put(16, [*three_terms(m), total])

    keys(0)
    for s in range(steps):
        loads[s][1].wait()
        loads[s][2].wait()
        if s + 1 < steps:
            keys(s + 1)
        for p in range(n):
            plane(s, p)


def attend(half, feat, embed, visible, w_query, w_key):
    frames, planes, rows = feat.shape[:3]
    c = w_key.shape[0]
    n = 2
    count = planes // 2
    steps = count // n
    hbm = pl.BlockSpec(memory_space=pltpu.HBM)
    return pl.pallas_call(
        functools.partial(attend_kernel, half),
        out_shape=[jax.ShapeDtypeStruct((count, 136, 128), bf16)] * 4,
        in_specs=[hbm] * 5,
        out_specs=[VM] * 4,
        scratch_shapes=[
            pltpu.VMEM((steps, frames, n, rows, 128), bf16),
            pltpu.VMEM((steps, n, rows, 128), bf16),
            pltpu.VMEM((steps, frames, n, 8, 128), jnp.int32),
            pltpu.VMEM((c, c), bf16),
            pltpu.VMEM((c, c), bf16),
            pltpu.VMEM((n, rows, 128), f32),
            pltpu.VMEM((n, rows, 128), f32),
            pltpu.SemaphoreType.DMA((steps + 1, 3)),
        ],
        compiler_params=pltpu.CompilerParams(vmem_limit_bytes=14 << 20),
        cost_estimate=pl.CostEstimate(flops=10**8, bytes_accessed=12 << 20, transcendentals=0),
        name="attend",
    )(feat, embed, visible, w_query, w_key)


def spread(v):
    u = v + pltpu.roll(v, 64, 1)
    return u + pltpu.roll(u, 32, 1)


def merged_plane(parts):
    lane = lax.broadcasted_iota(jnp.int32, (8, 128), 1)
    tail = lane >= 96
    stats = [r[p, 128:136, :].astype(f32) for r, p in parts]
    ms = [spread(jnp.where(tail, 0.0, s)) for s in stats]
    ls = [spread(jnp.where(tail, s, 0.0)) for s in stats]
    m = functools.reduce(jnp.maximum, ms)
    ws = [jnp.exp(v - m) for v in ms]
    total = sum(w * v for w, v in zip(ws, ls))
    return ws, total, m


def weighted_rows(parts, ws):
    acc = None
    for (r, p), w in zip(parts, ws):
        term = r[p, 0:128, :].astype(f32).reshape(16, 8, 128) * w[None]
        acc = term if acc is None else acc + term
    return acc.reshape(128, 128)


def merge_kernel(n, sizes, *refs):
    ins, outs = refs[:n], refs[n:]
    lane = lax.broadcasted_iota(jnp.int32, (8, 128), 1)
    at = 0
    for out, size in zip(outs, sizes):
        for i in range(size):
            parts = [(r, at) for r in ins]
            ws, total, m = merged_plane(parts)
            out[i, 0:128, :] = weighted_rows(parts, ws).astype(bf16)
            hi, mid, low = three_terms(m)
            packed = jnp.where(
                lane < 32, hi, jnp.where(lane < 64, mid, jnp.where(lane >= 96, total, low))
            )
            out[i, 128:136, :] = packed.astype(bf16)
            at += 1


def merge(parts, sizes):
    n = parts[0].shape[0]
    return pl.pallas_call(
        functools.partial(merge_kernel, len(parts), sizes),
        out_shape=[jax.ShapeDtypeStruct((s, 136, 128), bf16) for s in sizes],
        in_specs=[VM] * len(parts),
        out_specs=[VM] * len(sizes),
        compiler_params=pltpu.CompilerParams(vmem_limit_bytes=6 << 20),
        cost_estimate=pl.CostEstimate(flops=n * 10**5, bytes_accessed=n * 10**5, transcendentals=0),
        name="merge",
    )(*parts)


def gather_kernel(*refs):
    ins, out = refs[:6], refs[6]
    lane = lax.broadcasted_iota(jnp.int32, (8, 128), 1)
    zh = lax.axis_index("frame") // 4
    for rel in range(4):
        slot = (zh + rel) & 3
        for i in range(4):
            at = (4 * rel + i) & 7
            parts = [(r, at) for r in ins[3 * (rel // 2) : 3 * (rel // 2) + 3]]
            ws, total, m = merged_plane(parts)
            out[slot, i, 0:128, :] = weighted_rows(parts, ws).astype(bf16)
            hi, mid, low = three_terms(m)
            packed = jnp.where(
                lane < 32, hi, jnp.where(lane < 64, mid, jnp.where(lane >= 96, total, low))
            )
            out[slot, i, 128:136, :] = packed.astype(bf16)


def gather(*parts):
    return pl.pallas_call(
        gather_kernel,
        out_shape=jax.ShapeDtypeStruct((4, 4, 136, 128), bf16),
        in_specs=[VM] * 6,
        out_specs=VM,
        compiler_params=pltpu.CompilerParams(vmem_limit_bytes=6 << 20),
        name="gather",
    )(*parts)


def finish_kernel(part, wv, wo, out, rows):
    for p in range(4):
        parts = [(part.at[i], p) for i in range(4)]
        ws, total, _ = merged_plane(parts)
        inv = 1.0 / total
        rows[128 * p : 128 * p + 128, :] = weighted_rows(parts, [w * inv for w in ws])
    lines = []
    for x in range(8):
        t = rows[pl.ds(x, 64, stride=8), :].T
        lines.append(jnp.concatenate([t[32 * i : 32 * i + 32] for i in range(4)], axis=1))
    mixed = jnp.concatenate(lines, axis=0).astype(bf16)
    attended = dot(mixed, wv[...]).astype(bf16)
    out[...] = dot(attended, wo[...]).astype(bf16)


def finish(part, wv, wo):
    return pl.pallas_call(
        finish_kernel,
        out_shape=jax.ShapeDtypeStruct((256, 256), bf16),
        in_specs=[VM] * 3,
        out_specs=VM,
        scratch_shapes=[pltpu.VMEM((512, 128), f32)],
        compiler_params=pltpu.CompilerParams(vmem_limit_bytes=6 << 20),
        name="finish",
    )(part, wv, wo)


def weights_kernel(w, wv, wo, band, wide_v, wide_o, tmp):
    zero = jnp.zeros((64, 64), bf16)
    for tap in range(9):
        a = [w[0, 9 * i + tap] for i in range(3)]
        left = jnp.concatenate([a[0], a[1], a[2], zero], axis=0)
        right = jnp.concatenate([zero, a[0], a[1], a[2]], axis=0)
        e = tap % 3
        band[0, tap // 3, :, 128 * e : 128 * e + 128] = jnp.concatenate([left, right], axis=1)

    @pl.when(pl.program_id(0) == 0)
    def _():
        tmp[...] = wv[...].astype(f32)
        blank = jnp.zeros((16, 64), f32)
        for i in range(4):
            piece = tmp[pl.ds(i, 16, stride=4), :]
            for p in range(4):
                line = jnp.concatenate([piece if j == p else blank for j in range(4)], axis=1)
                at = 64 * i + 16 * p
                wide_v[at : at + 16, :] = line.astype(bf16)
        for p in range(4):
            line = jnp.concatenate([wo[...] if j == p else zero for j in range(4)], axis=1)
            wide_o[64 * p : 64 * p + 64, :] = line


def weights(conv_weight, w_value, w_out):
    layers = conv_weight.shape[0]
    small = pl.BlockSpec((64, 64), lambda i: (0, 0))
    big = pl.BlockSpec((256, 256), lambda i: (0, 0))
    return pl.pallas_call(
        weights_kernel,
        out_shape=[
            jax.ShapeDtypeStruct((layers, 3, 256, 384), bf16),
            jax.ShapeDtypeStruct((256, 256), bf16),
            jax.ShapeDtypeStruct((256, 256), bf16),
        ],
        grid=(layers,),
        in_specs=[pl.BlockSpec((1, 27, 64, 64), lambda i: (i, 0, 0, 0)), small, small],
        out_specs=[pl.BlockSpec((1, 3, 256, 384), lambda i: (i, 0, 0, 0)), big, big],
        scratch_shapes=[pltpu.VMEM((64, 64), f32)],
        compiler_params=pltpu.CompilerParams(
            dimension_semantics=("arbitrary",), vmem_limit_bytes=8 << 20
        ),
        cost_estimate=pl.CostEstimate(flops=10**6, bytes_accessed=8 << 20, transcendentals=0),
        name="weights",
    )(conv_weight.reshape(layers, 27, 64, 64), w_value, w_out)


def conv_kernel(block, band, bias, out, buf0, buf1, mask):
    layers = band.shape[0]
    me = lax.axis_index("frame")
    xi = me % 4
    x0, z0 = lax.axis_index("bx") * 8, me // 4 * 4
    y0 = lax.axis_index("by") * 128 + xi * 32
    y = lax.broadcasted_iota(jnp.int32, (stride, 128), 0) + (y0 - halo)
    y_ok = (y >= 0) & (y < 512)
    for x in range(16):
        x_at = x0 - halo + x
        line = jnp.where(y_ok & (x_at >= 0) & (x_at < 32), 1.0, 0.0)
        mask[stride * x : stride * x + stride, :] = line
    lane = lax.broadcasted_iota(jnp.int32, (1, 128), 1)
    for layer in range(layers):
        src = (block, buf0, buf1, buf0)[layer]
        dst = (buf0, buf1, buf0, None)[layer]
        first = stride * (layer + 1)
        n = stride * (14 - 2 * layer)

        def pair(t, carry, src=src, dst=dst, layer=layer, first=first, n=n):
            lanes_in = pl.ds(pl.multiple_of(128 * t, 128), 256)
            lanes_out = pl.ds(pl.multiple_of(128 * t, 128), 128)
            acc = None
            for b in range(3):
                rows = slice(first + stride * (b - 1), first + stride * (b - 1) + n)
                term = dot(src[rows, lanes_in], band[layer, b])
                acc = term if acc is None else acc + term
            h = acc[:, 128:256] + bias[layer : layer + 1, :]
            h = h + pltpu.roll(acc[:, 0:128], 1, 0) + pltpu.roll(acc[:, 256:384], n - 1, 0)
            if dst is None:
                h = pltpu.roll(h, n - halo, 0)
                tiles = [h[stride * x : stride * x + 32] for x in range(8)]
                whole = jnp.concatenate(tiles, axis=0).T.astype(bf16)
                for i in range(2):
                    out[(2 * t + i - xi) & 3] = whole[64 * i : 64 * i + 64]
            else:
                z = z0 - halo + layer + 1 + 2 * t + lane // 64
                ok = jnp.where((z >= 0) & (z < 16), 1.0, 0.0) * mask[first : first + n, :]
                dst[first : first + n, lanes_out] = jnp.where(
                    ok > 0, jnp.maximum(h, 0.0), 0.0
                ).astype(bf16)
            return carry

        lax.fori_loop(0, 5 - layer, pair, 0)


def convolve(block, band, bias):
    return pl.pallas_call(
        conv_kernel,
        out_shape=jax.ShapeDtypeStruct((4, 64, 256), bf16),
        in_specs=[VM, VM, VM],
        out_specs=VM,
        scratch_shapes=[
            pltpu.VMEM((16 * stride, 640), bf16),
            pltpu.VMEM((16 * stride, 512), bf16),
            pltpu.VMEM((16 * stride, 128), f32),
        ],
        compiler_params=pltpu.CompilerParams(vmem_limit_bytes=20 << 20),
        name="convolve",
    )(block, band, bias)


def place_kernel(own, high, far, low, out, rows):
    turn = 32 * (lax.axis_index("frame") % 4)
    parts = [r[...].astype(f32) for r in (own, high, far, low)]
    for x in range(8):
        line = jnp.concatenate([p[:, 32 * x : 32 * x + 32] for p in parts], axis=1)
        rows[pl.ds(x, 64, stride=8), :] = pltpu.roll(line, turn, 1)
    out[...] = rows[...].astype(bf16)


def place(own, high, far, low):
    return pl.pallas_call(
        place_kernel,
        out_shape=jax.ShapeDtypeStruct((512, 128), bf16),
        in_specs=[VM] * 4,
        out_specs=VM,
        scratch_shapes=[pltpu.VMEM((512, 128), f32)],
        compiler_params=pltpu.CompilerParams(vmem_limit_bytes=4 << 20),
        name="place",
    )(own, high, far, low)


def send(v, way, axis="frame"):
    return lax.ppermute(v, axis, way)


def joined(features, voxel_embed, visible, w_query, w_key, w_value, w_out, conv_weight, conv_bias):
    around = range(4)
    x_by = lambda k: [(4 * z + x, 4 * z + (x + k) % 4) for z in around for x in around]
    up, down = x_by(1), x_by(3)
    groups = [[4 * z + x for z in around] for x in around]
    frames, planes, c = features.shape[:3]
    feat = features.reshape(frames, planes, c * 8, 128)
    embed = voxel_embed.reshape(planes, c * 8, 128)
    a0, a1, a2, a3 = attend(0, feat, embed, visible, w_query, w_key)
    from_low = send(a2, up)
    high_a = send(a3, down)
    b0, b1, b2, b3 = attend(1, feat, embed, visible, w_query, w_key)
    band, wide_v, wide_o = weights(conv_weight, w_value, w_out)
    from_high = send(b2, down)
    low_b = send(b1, up)
    low_a = send(merge([a1, from_low], [8])[0], up)
    high_b = send(merge([b3, from_high], [8])[0], down)
    part = gather(a0, low_a, high_a, b0, low_b, high_b)
    part = lax.all_to_all(part, "frame", 0, 0, axis_index_groups=groups, tiled=True)
    hidden = finish(part, wide_v, wide_o).reshape(8, 32, 256)

    z_next = [(i, i + 4) for i in range(12)]
    z_prev = [(j, i) for i, j in z_next]
    below = send(hidden, z_next)
    above = send(hidden, z_prev)
    hidden = jnp.concatenate([below, hidden, above], axis=2)

    def where_is(z, chunk):
        return (4 * z + chunk % 4) * 4 + chunk // 4

    y_next = [(where_is(z, k), where_is(z, k + 1)) for z in range(4) for k in range(15)]
    y_prev = [(j, i) for i, j in y_next]
    left = send(hidden[:, -halo:], y_next, ("frame", "by"))
    right = send(hidden[:, :halo], y_prev, ("frame", "by"))
    hidden = jnp.concatenate([left, hidden, right], axis=1)
    x_next = [(0, 1), (1, 2), (2, 3)]
    x_prev = [(j, i) for i, j in x_next]
    front = send(hidden[-halo:], x_next, "bx")
    back = send(hidden[:halo], x_prev, "bx")
    pad = jnp.zeros((16, stride - 32 - 2 * halo, 768), bf16)
    hidden = jnp.concatenate([jnp.concatenate([front, hidden, back], axis=0), pad], axis=1)
    bias = jnp.concatenate([conv_bias, conv_bias], axis=1)
    out = convolve(hidden.reshape(16 * stride, 768), band, bias)
    low = send(out[1], up)
    high = send(out[3], down)
    far = send(out[2], x_by(2))
    return place(out[0], high, far, low).reshape(1, c, 8, 128)


def solution(mesh):
    return jax.shard_map(
        joined,
        mesh=mesh,
        in_specs=(
            P("frame", None, None, "bx", "by"),
            P(None, None, "bx", "by"),
            P("frame", None, "bx", "by"),
            P(),
            P(),
            P(),
            P(),
            P(),
            P(),
        ),
        out_specs=P("frame", None, "bx", "by"),
        check_vma=False,
    )
```

```python
import functools

import jax
import jax.numpy as jnp
from jax import lax
from jax.experimental import pallas as pl
from jax.experimental.pallas import tpu as pltpu
from jax.sharding import PartitionSpec as P


absent_score = -1e30
halo = 4
stride = 48
bf16, f32 = jnp.bfloat16, jnp.float32
VM = pl.BlockSpec(memory_space=pltpu.VMEM)


def dot(a, b):
    return jnp.dot(a, b, preferred_element_type=f32)


def lane_blocks(v):
    lane = lax.broadcasted_iota(jnp.int32, (8, 128), 1)
    low = lane < 64
    even = (lane & 63) < 32
    t = [None] * 4
    for i in (0, 1):
        t[i] = jnp.where(low, v[i], pltpu.roll(v[i + 2], 64, 1))
        t[i + 2] = jnp.where(low, pltpu.roll(v[i], 64, 1), v[i + 2])
    o = [None] * 4
    for i in (0, 2):
        o[i] = jnp.where(even, t[i], pltpu.roll(t[i + 1], 32, 1))
        o[i + 1] = jnp.where(even, pltpu.roll(t[i], 96, 1), t[i + 1])
    return o


def three_terms(m):
    hi = m.astype(bf16).astype(f32)
    mid = (m - hi).astype(bf16).astype(f32)
    return hi, mid, m - hi - mid


def attend_kernel(half, feat_at, embed_at, seen_at, wq_at, wk_at, *refs):
    outs, feat, embed, seen, wq, wk, key0, key1, sems = refs[:4], *refs[4:]
    steps, frames, n = feat.shape[:3]
    me = lax.axis_index("frame")
    zh, xi = me // 4, me % 4
    turn = (128 - 32 * xi) & 127

    def copies(s):
        block = 1 + 2 * half + s * n // 4
        z = pl.ds(((block + zh) & 3) * 4 + s * n % 4, n)
        return [
            pltpu.make_async_copy(embed_at.at[z], embed.at[s], sems.at[s, 0]),
            pltpu.make_async_copy(feat_at.at[:, z], feat.at[s], sems.at[s, 1]),
            pltpu.make_async_copy(seen_at.at[:, z], seen.at[s], sems.at[s, 2]),
        ]

    loads = [copies(s) for s in range(steps)]
    small = [
        pltpu.make_async_copy(wq_at, wq, sems.at[steps, 0]),
        pltpu.make_async_copy(wk_at, wk, sems.at[steps, 1]),
    ]
    for c in [loads[0][0], *small, *loads[0][1:], *sum(loads[1:], [])]:
        c.start()
    for c in small:
        c.wait()

    def keys(s):
        key = (key0, key1)[s % 2]
        loads[s][0].wait()
        for p in range(n):
            key[p] = embed[s, p].astype(f32)
        cols = [key[p, pl.ds(i, 64, stride=8), :] for p in range(n) for i in range(8)]
        wide = jnp.concatenate(cols, axis=1).astype(bf16)
        q = lax.dot_general(wq[...], wide, (((0,), (0,)), ((), ())), preferred_element_type=f32)
        qk = dot(wk[...], q.astype(bf16)) * 0.125
        for p in range(n):
            for i in range(8):
                at = (8 * p + i) * 128
                key[p, pl.ds(i, 64, stride=8), :] = qk[:, at : at + 128]

    def plane(s, p):
        key = (key0, key1)[s % 2]
        sums = [jnp.zeros((8, 128), f32) for _ in range(frames)]
        for g in range(16):
            rows = slice(32 * g, 32 * g + 32)
            line = key[p, rows, :]
            for f in range(frames):
                prod = (line * feat[s, f, p, rows, :].astype(f32)).reshape(4, 8, 128)
                sums[f] = sums[f] + jnp.sum(prod, axis=0)
        ok = [seen[s, f, p] > 0 for f in range(frames)]
        m = jnp.full((8, 128), absent_score, f32)
        for f in range(frames):
            m = jnp.maximum(m, jnp.where(ok[f], sums[f], absent_score))
        e = [jnp.where(ok[f], jnp.exp(sums[f] - m), 0.0) for f in range(frames)]
        total = e[0]
        for f in range(1, frames):
            total = total + e[f]

        def put(g, tiles):
            tiles = [pltpu.roll(t, turn, 1) for t in tiles]
            for out, tile in zip(outs, lane_blocks(tiles)):
                out[s * n + p, 8 * g : 8 * g + 8, :] = tile.astype(bf16)

        for g in range(16):
            rows = slice(32 * g, 32 * g + 32)
            acc = None
            for f in range(frames):
                term = e[f][None] * feat[s, f, p, rows, :].astype(f32).reshape(4, 8, 128)
                acc = term if acc is None else acc + term
            put(g, [acc[i] for i in range(4)])
        put(16, [*three_terms(m), total])

    keys(0)
    for s in range(steps):
        loads[s][1].wait()
        loads[s][2].wait()
        if s + 1 < steps:
            keys(s + 1)
        for p in range(n):
            plane(s, p)


def attend(half, feat, embed, visible, w_query, w_key):
    frames, planes, rows = feat.shape[:3]
    c = w_key.shape[0]
    n = 2
    count = planes // 2
    steps = count // n
    hbm = pl.BlockSpec(memory_space=pltpu.HBM)
    return pl.pallas_call(
        functools.partial(attend_kernel, half),
        out_shape=[jax.ShapeDtypeStruct((count, 136, 128), bf16)] * 4,
        in_specs=[hbm] * 5,
        out_specs=[VM] * 4,
        scratch_shapes=[
            pltpu.VMEM((steps, frames, n, rows, 128), bf16),
            pltpu.VMEM((steps, n, rows, 128), bf16),
            pltpu.VMEM((steps, frames, n, 8, 128), jnp.int32),
            pltpu.VMEM((c, c), bf16),
            pltpu.VMEM((c, c), bf16),
            pltpu.VMEM((n, rows, 128), f32),
            pltpu.VMEM((n, rows, 128), f32),
            pltpu.SemaphoreType.DMA((steps + 1, 3)),
        ],
        compiler_params=pltpu.CompilerParams(vmem_limit_bytes=14 << 20),
        cost_estimate=pl.CostEstimate(flops=10**8, bytes_accessed=12 << 20, transcendentals=0),
        name="attend",
    )(*[pltpu.with_memory_space_constraint(v, pltpu.HBM) for v in (feat, embed, visible, w_query, w_key)])


def spread(v):
    u = v + pltpu.roll(v, 64, 1)
    return u + pltpu.roll(u, 32, 1)


def merged_plane(parts):
    lane = lax.broadcasted_iota(jnp.int32, (8, 128), 1)
    tail = lane >= 96
    stats = [r[p, 128:136, :].astype(f32) for r, p in parts]
    ms = [spread(jnp.where(tail, 0.0, s)) for s in stats]
    ls = [spread(jnp.where(tail, s, 0.0)) for s in stats]
    m = functools.reduce(jnp.maximum, ms)
    ws = [jnp.exp(v - m) for v in ms]
    total = sum(w * v for w, v in zip(ws, ls))
    return ws, total, m


def weighted_rows(parts, ws):
    acc = None
    for (r, p), w in zip(parts, ws):
        term = r[p, 0:128, :].astype(f32).reshape(16, 8, 128) * w[None]
        acc = term if acc is None else acc + term
    return acc.reshape(128, 128)


def merge_plane(out, i, parts):
    lane = lax.broadcasted_iota(jnp.int32, (8, 128), 1)
    ws, total, m = merged_plane(parts)
    out[i, 0:128, :] = weighted_rows(parts, ws).astype(bf16)
    hi, mid, low = three_terms(m)
    packed = jnp.where(
        lane < 32, hi, jnp.where(lane < 64, mid, jnp.where(lane >= 96, total, low))
    )
    out[i, 128:136, :] = packed.astype(bf16)


def merge_kernel(n, sizes, *refs):
    ins, outs = refs[:n], refs[n:]
    at = 0
    for out, size in zip(outs, sizes):
        for i in range(size):
            merge_plane(out, i, [(r, at) for r in ins])
            at += 1


def merge(parts, sizes):
    n = parts[0].shape[0]
    return pl.pallas_call(
        functools.partial(merge_kernel, len(parts), sizes),
        out_shape=[jax.ShapeDtypeStruct((s, 136, 128), bf16) for s in sizes],
        in_specs=[VM] * len(parts),
        out_specs=[VM] * len(sizes),
        compiler_params=pltpu.CompilerParams(vmem_limit_bytes=6 << 20),
        cost_estimate=pl.CostEstimate(flops=n * 10**5, bytes_accessed=n * 10**5, transcendentals=0),
        name="merge",
    )(*parts)


def lift_kernel(at, slot, came, out):
    other = 2 - at
    out[other : other + 2] = slot[other : other + 2]
    for i in range(2):
        merge_plane(out, at + i, [(slot, at + i), (came, i)])


def lift(at, slot, came):
    return pl.pallas_call(
        functools.partial(lift_kernel, at),
        out_shape=jax.ShapeDtypeStruct(slot.shape, bf16),
        in_specs=[VM] * 2,
        out_specs=VM,
        compiler_params=pltpu.CompilerParams(vmem_limit_bytes=4 << 20),
        cost_estimate=pl.CostEstimate(flops=10**5, bytes_accessed=10**5, transcendentals=0),
        name="lift",
    )(slot, came)


def finish_kernel(own, low, high, wv, wo, out, rows):
    for p in range(4):
        parts = [(own, p), (low, p), (high, p)]
        ws, total, _ = merged_plane(parts)
        inv = 1.0 / total
        rows[128 * p : 128 * p + 128, :] = weighted_rows(parts, [w * inv for w in ws])
    lines = []
    for x in range(8):
        t = rows[pl.ds(x, 64, stride=8), :].T
        lines.append(jnp.concatenate([t[32 * i : 32 * i + 32] for i in range(4)], axis=1))
    mixed = jnp.concatenate(lines, axis=0).astype(bf16)
    attended = dot(mixed, wv[...]).astype(bf16)
    out[...] = dot(attended, wo[...]).astype(bf16)


def finish(own, low, high, wv, wo):
    return pl.pallas_call(
        finish_kernel,
        out_shape=jax.ShapeDtypeStruct((256, 256), bf16),
        in_specs=[VM] * 5,
        out_specs=VM,
        scratch_shapes=[pltpu.VMEM((512, 128), f32)],
        compiler_params=pltpu.CompilerParams(vmem_limit_bytes=6 << 20),
        name="finish",
    )(own, low, high, wv, wo)


def weights_kernel(w, wv, wo, band, wide_v, wide_o, tmp):
    zero = jnp.zeros((64, 64), bf16)
    for tap in range(9):
        a = [w[0, 9 * i + tap] for i in range(3)]
        left = jnp.concatenate([a[0], a[1], a[2], zero], axis=0)
        right = jnp.concatenate([zero, a[0], a[1], a[2]], axis=0)
        e = tap % 3
        band[0, tap // 3, :, 128 * e : 128 * e + 128] = jnp.concatenate([left, right], axis=1)

    @pl.when(pl.program_id(0) == 0)
    def _():
        tmp[...] = wv[...].astype(f32)
        blank = jnp.zeros((16, 64), f32)
        for i in range(4):
            piece = tmp[pl.ds(i, 16, stride=4), :]
            for p in range(4):
                line = jnp.concatenate([piece if j == p else blank for j in range(4)], axis=1)
                at = 64 * i + 16 * p
                wide_v[at : at + 16, :] = line.astype(bf16)
        for p in range(4):
            line = jnp.concatenate([wo[...] if j == p else zero for j in range(4)], axis=1)
            wide_o[64 * p : 64 * p + 64, :] = line


def weights(conv_weight, w_value, w_out):
    layers = conv_weight.shape[0]
    small = pl.BlockSpec((64, 64), lambda i: (0, 0))
    big = pl.BlockSpec((256, 256), lambda i: (0, 0))
    return pl.pallas_call(
        weights_kernel,
        out_shape=[
            jax.ShapeDtypeStruct((layers, 3, 256, 384), bf16),
            jax.ShapeDtypeStruct((256, 256), bf16),
            jax.ShapeDtypeStruct((256, 256), bf16),
        ],
        grid=(layers,),
        in_specs=[pl.BlockSpec((1, 27, 64, 64), lambda i: (i, 0, 0, 0)), small, small],
        out_specs=[pl.BlockSpec((1, 3, 256, 384), lambda i: (i, 0, 0, 0)), big, big],
        scratch_shapes=[pltpu.VMEM((64, 64), f32)],
        compiler_params=pltpu.CompilerParams(
            dimension_semantics=("arbitrary",), vmem_limit_bytes=8 << 20
        ),
        cost_estimate=pl.CostEstimate(flops=10**6, bytes_accessed=8 << 20, transcendentals=0),
        name="weights",
    )(conv_weight.reshape(layers, 27, 64, 64), w_value, w_out)


def conv_kernel(block, band, bias, out, buf0, buf1, mask):
    layers = band.shape[0]
    me = lax.axis_index("frame")
    xi = me % 4
    x0, z0 = lax.axis_index("bx") * 8, me // 4 * 4
    y0 = lax.axis_index("by") * 128 + xi * 32
    y = lax.broadcasted_iota(jnp.int32, (stride, 128), 0) + (y0 - halo)
    y_ok = (y >= 0) & (y < 512)
    for x in range(16):
        x_at = x0 - halo + x
        line = jnp.where(y_ok & (x_at >= 0) & (x_at < 32), 1.0, 0.0)
        mask[stride * x : stride * x + stride, :] = line
    lane = lax.broadcasted_iota(jnp.int32, (1, 128), 1)
    for layer in range(layers):
        src = (block, buf0, buf1, buf0)[layer]
        dst = (buf0, buf1, buf0, None)[layer]
        first = stride * (layer + 1)
        n = stride * (14 - 2 * layer)

        def pair(t, carry, src=src, dst=dst, layer=layer, first=first, n=n):
            lanes_in = pl.ds(pl.multiple_of(128 * t, 128), 256)
            lanes_out = pl.ds(pl.multiple_of(128 * t, 128), 128)
            acc = None
            for b in range(3):
                rows = slice(first + stride * (b - 1), first + stride * (b - 1) + n)
                term = dot(src[rows, lanes_in], band[layer, b])
                acc = term if acc is None else acc + term
            h = acc[:, 128:256] + bias[layer : layer + 1, :]
            h = h + pltpu.roll(acc[:, 0:128], 1, 0) + pltpu.roll(acc[:, 256:384], n - 1, 0)
            if dst is None:
                h = pltpu.roll(h, n - halo, 0)
                tiles = [h[stride * x : stride * x + 32] for x in range(8)]
                whole = jnp.concatenate(tiles, axis=0).T.astype(bf16)
                for i in range(2):
                    out[(2 * t + i - xi) & 3] = whole[64 * i : 64 * i + 64]
            else:
                z = z0 - halo + layer + 1 + 2 * t + lane // 64
                ok = jnp.where((z >= 0) & (z < 16), 1.0, 0.0) * mask[first : first + n, :]
                dst[first : first + n, lanes_out] = jnp.where(
                    ok > 0, jnp.maximum(h, 0.0), 0.0
                ).astype(bf16)
            return carry

        lax.fori_loop(0, 5 - layer, pair, 0)


def convolve(block, band, bias):
    return pl.pallas_call(
        conv_kernel,
        out_shape=jax.ShapeDtypeStruct((4, 64, 256), bf16),
        in_specs=[VM, VM, VM],
        out_specs=VM,
        scratch_shapes=[
            pltpu.VMEM((16 * stride, 640), bf16),
            pltpu.VMEM((16 * stride, 512), bf16),
            pltpu.VMEM((16 * stride, 128), f32),
        ],
        compiler_params=pltpu.CompilerParams(vmem_limit_bytes=20 << 20),
        name="convolve",
    )(block, band, bias)


def place_kernel(own, high, far, low, out, rows):
    turn = 32 * (lax.axis_index("frame") % 4)
    parts = [r[...].astype(f32) for r in (own, high, far, low)]
    for x in range(8):
        line = jnp.concatenate([p[:, 32 * x : 32 * x + 32] for p in parts], axis=1)
        rows[pl.ds(x, 64, stride=8), :] = pltpu.roll(line, turn, 1)
    out[...] = rows[...].astype(bf16)


def place(own, high, far, low):
    return pl.pallas_call(
        place_kernel,
        out_shape=jax.ShapeDtypeStruct((512, 128), bf16),
        in_specs=[VM] * 4,
        out_specs=VM,
        scratch_shapes=[pltpu.VMEM((512, 128), f32)],
        compiler_params=pltpu.CompilerParams(vmem_limit_bytes=4 << 20),
        name="place",
    )(own, high, far, low)


def send(v, way, axis="frame"):
    return lax.ppermute(v, axis, way)


def joined(features, voxel_embed, visible, w_query, w_key, w_value, w_out, conv_weight, conv_bias):
    around = range(4)
    x_by = lambda k: [(4 * z + x, 4 * z + (x + k) % 4) for z in around for x in around]
    up, down = x_by(1), x_by(3)
    z_up = [(i, (i + 4) % 16) for i in range(16)]
    z_down = [(j, i) for i, j in z_up]
    frames, planes, c = features.shape[:3]
    feat = features.reshape(frames, planes, c * 8, 128)
    embed = voxel_embed.reshape(planes, c * 8, 128)
    a0, a1, a2, a3 = attend(0, feat, embed, visible, w_query, w_key)
    from_low = send(a2, up)
    high_a = send(a3, down)
    b0, b1, b2, b3 = attend(1, feat, embed, visible, w_query, w_key)
    band, wide_v, wide_o = weights(conv_weight, w_value, w_out)
    from_high = send(b2, down)
    low_b = send(b1, up)
    low_a = send(merge([a1, from_low], [8])[0], up)
    high_b = send(merge([b3, from_high], [8])[0], down)
    z1, z2a, z2b = merge([a0, low_a, high_a], [4, 2, 2])
    from_low = send(z2a, z_up)
    from_high = send(z2b, z_down)
    low = send(lift(0, z1, from_low), z_up)
    z3, z0 = merge([b0, low_b, high_b], [4, 4])
    high = send(lift(2, z3, from_high), z_down)
    hidden = finish(z0, low, high, wide_v, wide_o).reshape(8, 32, 256)

    z_next = [(i, i + 4) for i in range(12)]
    z_prev = [(j, i) for i, j in z_next]
    below = send(hidden, z_next)
    above = send(hidden, z_prev)
    hidden = jnp.concatenate([below, hidden, above], axis=2)

    def where_is(z, chunk):
        return (4 * z + chunk % 4) * 4 + chunk // 4

    y_next = [(where_is(z, k), where_is(z, k + 1)) for z in range(4) for k in range(15)]
    y_prev = [(j, i) for i, j in y_next]
    left = send(hidden[:, -halo:], y_next, ("frame", "by"))
    right = send(hidden[:, :halo], y_prev, ("frame", "by"))
    hidden = jnp.concatenate([left, hidden, right], axis=1)
    x_next = [(0, 1), (1, 2), (2, 3)]
    x_prev = [(j, i) for i, j in x_next]
    front = send(hidden[-halo:], x_next, "bx")
    back = send(hidden[:halo], x_prev, "bx")
    pad = jnp.zeros((16, stride - 32 - 2 * halo, 768), bf16)
    hidden = jnp.concatenate([jnp.concatenate([front, hidden, back], axis=0), pad], axis=1)
    bias = jnp.concatenate([conv_bias, conv_bias], axis=1)
    out = convolve(hidden.reshape(16 * stride, 768), band, bias)
    low = send(out[1], up)
    high = send(out[3], down)
    far = send(out[2], x_by(2))
    return place(out[0], high, far, low).reshape(1, c, 8, 128)


def solution(mesh):
    return jax.shard_map(
        joined,
        mesh=mesh,
        in_specs=(
            P("frame", None, None, "bx", "by"),
            P(None, None, "bx", "by"),
            P("frame", None, "bx", "by"),
            P(),
            P(),
            P(),
            P(),
            P(),
            P(),
        ),
        out_specs=P("frame", None, "bx", "by"),
        check_vma=False,
    )
```

```python
import functools

import jax
import jax.numpy as jnp
from jax import lax
from jax.experimental import pallas as pl
from jax.experimental.pallas import tpu as pltpu
from jax.sharding import PartitionSpec as P


absent_score = -1e30
halo = 4
stride = 48
bf16, f32 = jnp.bfloat16, jnp.float32
VM = pl.BlockSpec(memory_space=pltpu.VMEM)


def dot(a, b):
    return jnp.dot(a, b, preferred_element_type=f32)


def lane_blocks(v):
    lane = lax.broadcasted_iota(jnp.int32, (8, 128), 1)
    low = lane < 64
    even = (lane & 63) < 32
    t = [None] * 4
    for i in (0, 1):
        t[i] = jnp.where(low, v[i], pltpu.roll(v[i + 2], 64, 1))
        t[i + 2] = jnp.where(low, pltpu.roll(v[i], 64, 1), v[i + 2])
    o = [None] * 4
    for i in (0, 2):
        o[i] = jnp.where(even, t[i], pltpu.roll(t[i + 1], 32, 1))
        o[i + 1] = jnp.where(even, pltpu.roll(t[i], 96, 1), t[i + 1])
    return o


def three_terms(m):
    hi = m.astype(bf16).astype(f32)
    mid = (m - hi).astype(bf16).astype(f32)
    return hi, mid, m - hi - mid


def attend_kernel(half, feat_at, embed_at, seen_at, wq_at, wk_at, *refs):
    outs, feat, embed, seen, wq, wk, key0, key1, sems = refs[:4], *refs[4:]
    steps, frames, n = feat.shape[:3]
    me = lax.axis_index("frame")
    zh, xi = me // 4, me % 4
    turn = (128 - 32 * xi) & 127

    def copies(s):
        block = 1 + 2 * half + s * n // 4
        z = pl.ds(((block + zh) & 3) * 4 + s * n % 4, n)
        return [
            pltpu.make_async_copy(embed_at.at[z], embed.at[s], sems.at[s, 0]),
            pltpu.make_async_copy(feat_at.at[:, z], feat.at[s], sems.at[s, 1]),
            pltpu.make_async_copy(seen_at.at[:, z], seen.at[s], sems.at[s, 2]),
        ]

    loads = [copies(s) for s in range(steps)]
    small = [
        pltpu.make_async_copy(wq_at, wq, sems.at[steps, 0]),
        pltpu.make_async_copy(wk_at, wk, sems.at[steps, 1]),
    ]
    for c in [loads[0][0], *small, *loads[0][1:], *sum(loads[1:], [])]:
        c.start()
    for c in small:
        c.wait()

    def keys(s):
        key = (key0, key1)[s % 2]
        loads[s][0].wait()
        for p in range(n):
            key[p] = embed[s, p].astype(f32)
        cols = [key[p, pl.ds(i, 64, stride=8), :] for p in range(n) for i in range(8)]
        wide = jnp.concatenate(cols, axis=1).astype(bf16)
        q = lax.dot_general(wq[...], wide, (((0,), (0,)), ((), ())), preferred_element_type=f32)
        qk = dot(wk[...], q.astype(bf16)) * 0.125
        for p in range(n):
            for i in range(8):
                at = (8 * p + i) * 128
                key[p, pl.ds(i, 64, stride=8), :] = qk[:, at : at + 128]

    def plane(s, p):
        key = (key0, key1)[s % 2]
        sums = [jnp.zeros((8, 128), f32) for _ in range(frames)]
        for g in range(16):
            rows = slice(32 * g, 32 * g + 32)
            line = key[p, rows, :]
            for f in range(frames):
                prod = (line * feat[s, f, p, rows, :].astype(f32)).reshape(4, 8, 128)
                sums[f] = sums[f] + jnp.sum(prod, axis=0)
        ok = [seen[s, f, p] > 0 for f in range(frames)]
        m = jnp.full((8, 128), absent_score, f32)
        for f in range(frames):
            m = jnp.maximum(m, jnp.where(ok[f], sums[f], absent_score))
        e = [jnp.where(ok[f], jnp.exp(sums[f] - m), 0.0) for f in range(frames)]
        total = e[0]
        for f in range(1, frames):
            total = total + e[f]

        def put(g, tiles):
            tiles = [pltpu.roll(t, turn, 1) for t in tiles]
            for out, tile in zip(outs, lane_blocks(tiles)):
                out[s * n + p, 8 * g : 8 * g + 8, :] = tile.astype(bf16)

        for g in range(16):
            rows = slice(32 * g, 32 * g + 32)
            acc = None
            for f in range(frames):
                term = e[f][None] * feat[s, f, p, rows, :].astype(f32).reshape(4, 8, 128)
                acc = term if acc is None else acc + term
            put(g, [acc[i] for i in range(4)])
        put(16, [*three_terms(m), total])

    keys(0)
    for s in range(steps):
        loads[s][1].wait()
        loads[s][2].wait()
        if s + 1 < steps:
            keys(s + 1)
        for p in range(n):
            plane(s, p)


def attend(half, feat, embed, visible, w_query, w_key):
    frames, planes, rows = feat.shape[:3]
    c = w_key.shape[0]
    n = 2
    count = planes // 2
    steps = count // n
    hbm = pl.BlockSpec(memory_space=pltpu.HBM)
    return pl.pallas_call(
        functools.partial(attend_kernel, half),
        out_shape=[jax.ShapeDtypeStruct((count, 136, 128), bf16)] * 4,
        in_specs=[hbm] * 5,
        out_specs=[VM] * 4,
        scratch_shapes=[
            pltpu.VMEM((steps, frames, n, rows, 128), bf16),
            pltpu.VMEM((steps, n, rows, 128), bf16),
            pltpu.VMEM((steps, frames, n, 8, 128), jnp.int32),
            pltpu.VMEM((c, c), bf16),
            pltpu.VMEM((c, c), bf16),
            pltpu.VMEM((n, rows, 128), f32),
            pltpu.VMEM((n, rows, 128), f32),
            pltpu.SemaphoreType.DMA((steps + 1, 3)),
        ],
        compiler_params=pltpu.CompilerParams(vmem_limit_bytes=14 << 20),
        cost_estimate=pl.CostEstimate(flops=10**8, bytes_accessed=12 << 20, transcendentals=0),
        name="attend",
    )(*[pltpu.with_memory_space_constraint(v, pltpu.HBM) for v in (feat, embed, visible, w_query, w_key)])


def spread(v):
    u = v + pltpu.roll(v, 64, 1)
    return u + pltpu.roll(u, 32, 1)


def merged_plane(parts):
    lane = lax.broadcasted_iota(jnp.int32, (8, 128), 1)
    tail = lane >= 96
    stats = [r[p, 128:136, :].astype(f32) for r, p in parts]
    ms = [spread(jnp.where(tail, 0.0, s)) for s in stats]
    ls = [spread(jnp.where(tail, s, 0.0)) for s in stats]
    m = functools.reduce(jnp.maximum, ms)
    ws = [jnp.exp(v - m) for v in ms]
    total = sum(w * v for w, v in zip(ws, ls))
    return ws, total, m


def weighted_rows(parts, ws):
    acc = None
    for (r, p), w in zip(parts, ws):
        term = r[p, 0:128, :].astype(f32).reshape(16, 8, 128) * w[None]
        acc = term if acc is None else acc + term
    return acc.reshape(128, 128)


def merge_plane(out, i, parts):
    lane = lax.broadcasted_iota(jnp.int32, (8, 128), 1)
    ws, total, m = merged_plane(parts)
    out[i, 0:128, :] = weighted_rows(parts, ws).astype(bf16)
    hi, mid, low = three_terms(m)
    packed = jnp.where(
        lane < 32, hi, jnp.where(lane < 64, mid, jnp.where(lane >= 96, total, low))
    )
    out[i, 128:136, :] = packed.astype(bf16)


def merge_kernel(n, sizes, *refs):
    ins, outs = refs[:n], refs[n:]
    at = 0
    for out, size in zip(outs, sizes):
        for i in range(size):
            merge_plane(out, i, [(r, at) for r in ins])
            at += 1


def merge(parts, sizes):
    n = parts[0].shape[0]
    return pl.pallas_call(
        functools.partial(merge_kernel, len(parts), sizes),
        out_shape=[jax.ShapeDtypeStruct((s, 136, 128), bf16) for s in sizes],
        in_specs=[VM] * len(parts),
        out_specs=[VM] * len(sizes),
        compiler_params=pltpu.CompilerParams(vmem_limit_bytes=6 << 20),
        cost_estimate=pl.CostEstimate(flops=n * 10**5, bytes_accessed=n * 10**5, transcendentals=0),
        name="merge",
    )(*parts)


def lift_kernel(at, slot, came, out):
    other = 2 - at
    out[other : other + 2] = slot[other : other + 2]
    for i in range(2):
        merge_plane(out, at + i, [(slot, at + i), (came, i)])


def lift(at, slot, came):
    return pl.pallas_call(
        functools.partial(lift_kernel, at),
        out_shape=jax.ShapeDtypeStruct(slot.shape, bf16),
        in_specs=[VM] * 2,
        out_specs=VM,
        compiler_params=pltpu.CompilerParams(vmem_limit_bytes=4 << 20),
        cost_estimate=pl.CostEstimate(flops=10**5, bytes_accessed=10**5, transcendentals=0),
        name="lift",
    )(slot, came)


def finish_kernel(own, low, high, wv, wo, out, rows):
    for p in range(4):
        parts = [(own, p), (low, p), (high, p)]
        ws, total, _ = merged_plane(parts)
        inv = 1.0 / total
        rows[128 * p : 128 * p + 128, :] = weighted_rows(parts, [w * inv for w in ws])
    lines = []
    for x in range(8):
        t = rows[pl.ds(x, 64, stride=8), :].T
        lines.append(jnp.concatenate([t[32 * i : 32 * i + 32] for i in range(4)], axis=1))
    mixed = jnp.concatenate(lines, axis=0).astype(bf16)
    attended = dot(mixed, wv[...]).astype(bf16)
    out[...] = dot(attended, wo[...]).astype(bf16)


def finish(own, low, high, wv, wo):
    return pl.pallas_call(
        finish_kernel,
        out_shape=jax.ShapeDtypeStruct((256, 256), bf16),
        in_specs=[VM] * 5,
        out_specs=VM,
        scratch_shapes=[pltpu.VMEM((512, 128), f32)],
        compiler_params=pltpu.CompilerParams(vmem_limit_bytes=6 << 20),
        name="finish",
    )(own, low, high, wv, wo)


def weights_kernel(w, wv, wo, band, wide_v, wide_o, tmp):
    zero = jnp.zeros((64, 64), bf16)
    for tap in range(9):
        a = [w[0, 9 * i + tap] for i in range(3)]
        left = jnp.concatenate([a[0], a[1], a[2], zero], axis=0)
        right = jnp.concatenate([zero, a[0], a[1], a[2]], axis=0)
        e = tap % 3
        band[0, tap // 3, :, 128 * e : 128 * e + 128] = jnp.concatenate([left, right], axis=1)

    @pl.when(pl.program_id(0) == 0)
    def _():
        tmp[...] = wv[...].astype(f32)
        blank = jnp.zeros((16, 64), f32)
        for i in range(4):
            piece = tmp[pl.ds(i, 16, stride=4), :]
            for p in range(4):
                line = jnp.concatenate([piece if j == p else blank for j in range(4)], axis=1)
                at = 64 * i + 16 * p
                wide_v[at : at + 16, :] = line.astype(bf16)
        for p in range(4):
            line = jnp.concatenate([wo[...] if j == p else zero for j in range(4)], axis=1)
            wide_o[64 * p : 64 * p + 64, :] = line


def weights(conv_weight, w_value, w_out):
    layers = conv_weight.shape[0]
    small = pl.BlockSpec((64, 64), lambda i: (0, 0))
    big = pl.BlockSpec((256, 256), lambda i: (0, 0))
    return pl.pallas_call(
        weights_kernel,
        out_shape=[
            jax.ShapeDtypeStruct((layers, 3, 256, 384), bf16),
            jax.ShapeDtypeStruct((256, 256), bf16),
            jax.ShapeDtypeStruct((256, 256), bf16),
        ],
        grid=(layers,),
        in_specs=[pl.BlockSpec((1, 27, 64, 64), lambda i: (i, 0, 0, 0)), small, small],
        out_specs=[pl.BlockSpec((1, 3, 256, 384), lambda i: (i, 0, 0, 0)), big, big],
        scratch_shapes=[pltpu.VMEM((64, 64), f32)],
        compiler_params=pltpu.CompilerParams(
            dimension_semantics=("arbitrary",), vmem_limit_bytes=8 << 20
        ),
        cost_estimate=pl.CostEstimate(flops=10**6, bytes_accessed=8 << 20, transcendentals=0),
        name="weights",
    )(conv_weight.reshape(layers, 27, 64, 64), w_value, w_out)


def conv_kernel(block, band, bias, out, buf0, buf1, mask):
    layers = band.shape[0]
    me = lax.axis_index("frame")
    xi = me % 4
    x0, z0 = lax.axis_index("bx") * 8, me // 4 * 4
    y0 = lax.axis_index("by") * 128 + xi * 32
    y = lax.broadcasted_iota(jnp.int32, (stride, 128), 0) + (y0 - halo)
    y_ok = (y >= 0) & (y < 512)
    for x in range(16):
        x_at = x0 - halo + x
        line = jnp.where(y_ok & (x_at >= 0) & (x_at < 32), 1.0, 0.0)
        mask[stride * x : stride * x + stride, :] = line
    lane = lax.broadcasted_iota(jnp.int32, (1, 128), 1)
    for layer in range(layers):
        src = (block, buf0, buf1, buf0)[layer]
        dst = (buf0, buf1, buf0, None)[layer]
        first = stride * (layer + 1)
        n = stride * (14 - 2 * layer)

        for t in range(5 - layer):
            acc = None
            for b in range(3):
                rows = slice(first + stride * (b - 1), first + stride * (b - 1) + n)
                term = dot(src[rows, 128 * t : 128 * t + 256], band[layer, b])
                acc = term if acc is None else acc + term
            h = acc[:, 128:256] + bias[layer : layer + 1, :]
            h = h + pltpu.roll(acc[:, 0:128], 1, 0) + pltpu.roll(acc[:, 256:384], n - 1, 0)
            if dst is None:
                h = pltpu.roll(h, n - halo, 0)
                tiles = [h[stride * x : stride * x + 32] for x in range(8)]
                whole = jnp.concatenate(tiles, axis=0).T.astype(bf16)
                for i in range(2):
                    out[(2 * t + i - xi) & 3] = whole[64 * i : 64 * i + 64]
            else:
                z = z0 - halo + layer + 1 + 2 * t + lane // 64
                ok = jnp.where((z >= 0) & (z < 16), 1.0, 0.0) * mask[first : first + n, :]
                dst[first : first + n, 128 * t : 128 * t + 128] = jnp.where(
                    ok > 0, jnp.maximum(h, 0.0), 0.0
                ).astype(bf16)


def convolve(block, band, bias):
    return pl.pallas_call(
        conv_kernel,
        out_shape=jax.ShapeDtypeStruct((4, 64, 256), bf16),
        in_specs=[VM, VM, VM],
        out_specs=VM,
        scratch_shapes=[
            pltpu.VMEM((16 * stride, 640), bf16),
            pltpu.VMEM((16 * stride, 512), bf16),
            pltpu.VMEM((16 * stride, 128), f32),
        ],
        compiler_params=pltpu.CompilerParams(vmem_limit_bytes=20 << 20),
        name="convolve",
    )(block, band, bias)


def place_kernel(own, high, far, low, out, rows):
    turn = 32 * (lax.axis_index("frame") % 4)
    parts = [r[...].astype(f32) for r in (own, high, far, low)]
    for x in range(8):
        line = jnp.concatenate([p[:, 32 * x : 32 * x + 32] for p in parts], axis=1)
        rows[pl.ds(x, 64, stride=8), :] = pltpu.roll(line, turn, 1)
    out[...] = rows[...].astype(bf16)


def place(own, high, far, low):
    return pl.pallas_call(
        place_kernel,
        out_shape=jax.ShapeDtypeStruct((512, 128), bf16),
        in_specs=[VM] * 4,
        out_specs=VM,
        scratch_shapes=[pltpu.VMEM((512, 128), f32)],
        compiler_params=pltpu.CompilerParams(vmem_limit_bytes=4 << 20),
        name="place",
    )(own, high, far, low)


def send(v, way, axis="frame"):
    return lax.ppermute(v, axis, way)


def only(inside, v):
    return jnp.where(inside, v, jnp.zeros_like(v))


def joined(features, voxel_embed, visible, w_query, w_key, w_value, w_out, conv_weight, conv_bias):
    around = range(4)
    x_by = lambda k: [(4 * z + x, 4 * z + (x + k) % 4) for z in around for x in around]
    up, down = x_by(1), x_by(3)
    z_up = [(i, (i + 4) % 16) for i in range(16)]
    z_down = [(j, i) for i, j in z_up]
    frames, planes, c = features.shape[:3]
    feat = features.reshape(frames, planes, c * 8, 128)
    embed = voxel_embed.reshape(planes, c * 8, 128)
    a0, a1, a2, a3 = attend(0, feat, embed, visible, w_query, w_key)
    from_low = send(a2, up)
    high_a = send(a3, down)
    b0, b1, b2, b3 = attend(1, feat, embed, visible, w_query, w_key)
    band, wide_v, wide_o = weights(conv_weight, w_value, w_out)
    from_high = send(b2, down)
    low_b = send(b1, up)
    low_a = send(merge([a1, from_low], [8])[0], up)
    high_b = send(merge([b3, from_high], [8])[0], down)
    z1, z2a, z2b = merge([a0, low_a, high_a], [4, 2, 2])
    from_low = send(z2a, z_up)
    from_high = send(z2b, z_down)
    low = send(lift(0, z1, from_low), z_up)
    z3, z0 = merge([b0, low_b, high_b], [4, 4])
    high = send(lift(2, z3, from_high), z_down)
    hidden = finish(z0, low, high, wide_v, wide_o).reshape(8, 32, 256)

    me = lax.axis_index("frame")
    zh, xi = me // 4, me % 4
    below = only(zh > 0, send(hidden, z_up))
    above = only(zh < 3, send(hidden, z_down))
    hidden = jnp.concatenate([below, hidden, above], axis=2)

    def where_is(z, chunk):
        return (4 * z + chunk % 4) * 4 + chunk // 4

    y_next = [(where_is(z, k), where_is(z, (k + 1) % 16)) for z in range(4) for k in range(16)]
    y_prev = [(j, i) for i, j in y_next]
    chunk = lax.axis_index("by") * 4 + xi
    left = only(chunk > 0, send(hidden[:, -halo:], y_next, ("frame", "by")))
    right = only(chunk < 15, send(hidden[:, :halo], y_prev, ("frame", "by")))
    hidden = jnp.concatenate([left, hidden, right], axis=1)
    x_next = [(i, (i + 1) % 4) for i in range(4)]
    x_prev = [(j, i) for i, j in x_next]
    bx = lax.axis_index("bx")
    front = only(bx > 0, send(hidden[-halo:], x_next, "bx"))
    back = only(bx < 3, send(hidden[:halo], x_prev, "bx"))
    pad = jnp.zeros((16, stride - 32 - 2 * halo, 768), bf16)
    hidden = jnp.concatenate([jnp.concatenate([front, hidden, back], axis=0), pad], axis=1)
    bias = jnp.concatenate([conv_bias, conv_bias], axis=1)
    out = convolve(hidden.reshape(16 * stride, 768), band, bias)
    low = send(out[1], up)
    high = send(out[3], down)
    far = send(out[2], x_by(2))
    return place(out[0], high, far, low).reshape(1, c, 8, 128)


def solution(mesh):
    return jax.shard_map(
        joined,
        mesh=mesh,
        in_specs=(
            P("frame", None, None, "bx", "by"),
            P(None, None, "bx", "by"),
            P("frame", None, "bx", "by"),
            P(),
            P(),
            P(),
            P(),
            P(),
            P(),
        ),
        out_specs=P("frame", None, "bx", "by"),
        check_vma=False,
    )
```

```python
import functools

import jax
import jax.numpy as jnp
from jax import lax
from jax.experimental import pallas as pl
from jax.experimental.pallas import tpu as pltpu
from jax.sharding import PartitionSpec as P


absent_score = -1e30
halo = 4
stride = 48
bf16, f32 = jnp.bfloat16, jnp.float32
VM = pl.BlockSpec(memory_space=pltpu.VMEM)


def dot(a, b):
    return jnp.dot(a, b, preferred_element_type=f32)


def lane_blocks(v):
    lane = lax.broadcasted_iota(jnp.int32, (8, 128), 1)
    low = lane < 64
    even = (lane & 63) < 32
    t = [None] * 4
    for i in (0, 1):
        t[i] = jnp.where(low, v[i], pltpu.roll(v[i + 2], 64, 1))
        t[i + 2] = jnp.where(low, pltpu.roll(v[i], 64, 1), v[i + 2])
    o = [None] * 4
    for i in (0, 2):
        o[i] = jnp.where(even, t[i], pltpu.roll(t[i + 1], 32, 1))
        o[i + 1] = jnp.where(even, pltpu.roll(t[i], 96, 1), t[i + 1])
    return o


def three_terms(m):
    hi = m.astype(bf16).astype(f32)
    mid = (m - hi).astype(bf16).astype(f32)
    return hi, mid, m - hi - mid


def attend_kernel(half, feat_at, embed_at, seen_at, wq_at, wk_at, *refs):
    outs, feat, embed, seen, wq, wk, key0, key1, wide0, wide1, sems = refs[:4], *refs[4:]
    steps, frames, n = feat.shape[:3]
    me = lax.axis_index("frame")
    zh, xi = me // 4, me % 4
    turn = (128 - 32 * xi) & 127

    def copies(s):
        block = 1 + 2 * half + s * n // 4
        z = pl.ds(((block + zh) & 3) * 4 + s * n % 4, n)
        return [
            pltpu.make_async_copy(embed_at.at[z], embed.at[s], sems.at[s, 0]),
            pltpu.make_async_copy(feat_at.at[:, z], feat.at[s], sems.at[s, 1]),
            pltpu.make_async_copy(seen_at.at[:, z], seen.at[s], sems.at[s, 2]),
        ]

    loads = [copies(s) for s in range(steps)]
    small = [
        pltpu.make_async_copy(wq_at, wq, sems.at[steps, 0]),
        pltpu.make_async_copy(wk_at, wk, sems.at[steps, 1]),
    ]
    for c in [loads[0][0], *small, *loads[0][1:], *sum(loads[1:], [])]:
        c.start()
    for c in small:
        c.wait()

    def keys(s):
        key = (key0, key1)[s % 2]
        loads[s][0].wait()
        for p in range(n):
            key[p] = embed[s, p].astype(f32)
        cols = [key[p, pl.ds(i, 64, stride=8), :] for p in range(n) for i in range(8)]
        wide = jnp.concatenate(cols, axis=1).astype(bf16)
        q = lax.dot_general(wq[...], wide, (((0,), (0,)), ((), ())), preferred_element_type=f32)
        qk = dot(wk[...], q.astype(bf16))
        for p in range(n):
            for i in range(8):
                at = (8 * p + i) * 128
                key[p, pl.ds(i, 64, stride=8), :] = qk[:, at : at + 128]

    def plane(s, p):
        key, wide = (key0, key1)[s % 2], (wide0, wide1)[p % 2]
        sums = [jnp.zeros((8, 128), f32) for _ in range(frames)]
        for g in range(16):
            rows = slice(32 * g, 32 * g + 32)
            line = key[p, rows, :]
            for f in range(frames):
                value = feat[s, f, p, rows, :].astype(f32)
                wide[f, rows, :] = value
                sums[f] = sums[f] + jnp.sum((line * value).reshape(4, 8, 128), axis=0)
        sums = [v * 0.125 for v in sums]
        ok = [seen[s, f, p] > 0 for f in range(frames)]
        m = jnp.full((8, 128), absent_score, f32)
        for f in range(frames):
            m = jnp.maximum(m, jnp.where(ok[f], sums[f], absent_score))
        e = [jnp.where(ok[f], jnp.exp(sums[f] - m), 0.0) for f in range(frames)]
        total = e[0]
        for f in range(1, frames):
            total = total + e[f]

        def put(g, tiles):
            tiles = [pltpu.roll(t, turn, 1) for t in tiles]
            for out, tile in zip(outs, lane_blocks(tiles)):
                out[s * n + p, 8 * g : 8 * g + 8, :] = tile.astype(bf16)

        for g in range(16):
            rows = slice(32 * g, 32 * g + 32)
            acc = None
            for f in range(frames):
                term = e[f][None] * wide[f, rows, :].reshape(4, 8, 128)
                acc = term if acc is None else acc + term
            put(g, [acc[i] for i in range(4)])
        put(16, [*three_terms(m), total])

    keys(0)
    for s in range(steps):
        loads[s][1].wait()
        loads[s][2].wait()
        if s + 1 < steps:
            keys(s + 1)
        for p in range(n):
            plane(s, p)


def attend(half, feat, embed, visible, w_query, w_key):
    frames, planes, rows = feat.shape[:3]
    c = w_key.shape[0]
    n = 2
    count = planes // 2
    steps = count // n
    hbm = pl.BlockSpec(memory_space=pltpu.HBM)
    return pl.pallas_call(
        functools.partial(attend_kernel, half),
        out_shape=[jax.ShapeDtypeStruct((count, 136, 128), bf16)] * 4,
        in_specs=[hbm] * 5,
        out_specs=[VM] * 4,
        scratch_shapes=[
            pltpu.VMEM((steps, frames, n, rows, 128), bf16),
            pltpu.VMEM((steps, n, rows, 128), bf16),
            pltpu.VMEM((steps, frames, n, 8, 128), jnp.int32),
            pltpu.VMEM((c, c), bf16),
            pltpu.VMEM((c, c), bf16),
            pltpu.VMEM((n, rows, 128), f32),
            pltpu.VMEM((n, rows, 128), f32),
            pltpu.VMEM((frames, rows, 128), f32),
            pltpu.VMEM((frames, rows, 128), f32),
            pltpu.SemaphoreType.DMA((steps + 1, 3)),
        ],
        compiler_params=pltpu.CompilerParams(vmem_limit_bytes=16 << 20),
        cost_estimate=pl.CostEstimate(flops=10**8, bytes_accessed=12 << 20, transcendentals=0),
        name="attend",
    )(*[pltpu.with_memory_space_constraint(v, pltpu.HBM) for v in (feat, embed, visible, w_query, w_key)])


def spread(v):
    u = v + pltpu.roll(v, 64, 1)
    return u + pltpu.roll(u, 32, 1)


def merged_plane(parts):
    lane = lax.broadcasted_iota(jnp.int32, (8, 128), 1)
    tail = lane >= 96
    stats = [r[p, 128:136, :].astype(f32) for r, p in parts]
    ms = [spread(jnp.where(tail, 0.0, s)) for s in stats]
    ls = [spread(jnp.where(tail, s, 0.0)) for s in stats]
    m = functools.reduce(jnp.maximum, ms)
    ws = [jnp.exp(v - m) for v in ms]
    total = sum(w * v for w, v in zip(ws, ls))
    return ws, total, m


def weighted_rows(parts, ws):
    acc = None
    for (r, p), w in zip(parts, ws):
        term = r[p, 0:128, :].astype(f32).reshape(16, 8, 128) * w[None]
        acc = term if acc is None else acc + term
    return acc.reshape(128, 128)


def merge_plane(out, i, parts):
    lane = lax.broadcasted_iota(jnp.int32, (8, 128), 1)
    ws, total, m = merged_plane(parts)
    out[i, 0:128, :] = weighted_rows(parts, ws).astype(bf16)
    hi, mid, low = three_terms(m)
    packed = jnp.where(
        lane < 32, hi, jnp.where(lane < 64, mid, jnp.where(lane >= 96, total, low))
    )
    out[i, 128:136, :] = packed.astype(bf16)


def merge_kernel(n, sizes, *refs):
    ins, outs = refs[:n], refs[n:]
    at = 0
    for out, size in zip(outs, sizes):
        for i in range(size):
            merge_plane(out, i, [(r, at) for r in ins])
            at += 1


def merge(parts, sizes):
    n = parts[0].shape[0]
    return pl.pallas_call(
        functools.partial(merge_kernel, len(parts), sizes),
        out_shape=[jax.ShapeDtypeStruct((s, 136, 128), bf16) for s in sizes],
        in_specs=[VM] * len(parts),
        out_specs=[VM] * len(sizes),
        compiler_params=pltpu.CompilerParams(vmem_limit_bytes=6 << 20),
        cost_estimate=pl.CostEstimate(flops=n * 10**5, bytes_accessed=n * 10**5, transcendentals=0),
        name="merge",
    )(*parts)


def lift_kernel(at, slot, came, out):
    other = 2 - at
    out[other : other + 2] = slot[other : other + 2]
    for i in range(2):
        merge_plane(out, at + i, [(slot, at + i), (came, i)])


def lift(at, slot, came):
    return pl.pallas_call(
        functools.partial(lift_kernel, at),
        out_shape=jax.ShapeDtypeStruct(slot.shape, bf16),
        in_specs=[VM] * 2,
        out_specs=VM,
        compiler_params=pltpu.CompilerParams(vmem_limit_bytes=4 << 20),
        cost_estimate=pl.CostEstimate(flops=10**5, bytes_accessed=10**5, transcendentals=0),
        name="lift",
    )(slot, came)


def finish_kernel(own, low, high, wv, wo, out, rows):
    for p in range(4):
        parts = [(own, p), (low, p), (high, p)]
        ws, total, _ = merged_plane(parts)
        inv = 1.0 / total
        rows[128 * p : 128 * p + 128, :] = weighted_rows(parts, [w * inv for w in ws])
    lines = []
    for x in range(8):
        t = rows[pl.ds(x, 64, stride=8), :].T
        lines.append(jnp.concatenate([t[32 * i : 32 * i + 32] for i in range(4)], axis=1))
    mixed = jnp.concatenate(lines, axis=0).astype(bf16)
    attended = dot(mixed, wv[...]).astype(bf16)
    out[...] = dot(attended, wo[...]).astype(bf16)


def finish(own, low, high, wv, wo):
    return pl.pallas_call(
        finish_kernel,
        out_shape=jax.ShapeDtypeStruct((256, 256), bf16),
        in_specs=[VM] * 5,
        out_specs=VM,
        scratch_shapes=[pltpu.VMEM((512, 128), f32)],
        compiler_params=pltpu.CompilerParams(vmem_limit_bytes=6 << 20),
        name="finish",
    )(own, low, high, wv, wo)


def weights_kernel(w, wv, wo, band, wide_v, wide_o, tmp):
    zero = jnp.zeros((64, 64), bf16)
    for tap in range(9):
        a = [w[0, 9 * i + tap] for i in range(3)]
        left = jnp.concatenate([a[0], a[1], a[2], zero], axis=0)
        right = jnp.concatenate([zero, a[0], a[1], a[2]], axis=0)
        e = tap % 3
        band[0, tap // 3, :, 128 * e : 128 * e + 128] = jnp.concatenate([left, right], axis=1)

    @pl.when(pl.program_id(0) == 0)
    def _():
        tmp[...] = wv[...].astype(f32)
        blank = jnp.zeros((16, 64), f32)
        for i in range(4):
            piece = tmp[pl.ds(i, 16, stride=4), :]
            for p in range(4):
                line = jnp.concatenate([piece if j == p else blank for j in range(4)], axis=1)
                at = 64 * i + 16 * p
                wide_v[at : at + 16, :] = line.astype(bf16)
        for p in range(4):
            line = jnp.concatenate([wo[...] if j == p else zero for j in range(4)], axis=1)
            wide_o[64 * p : 64 * p + 64, :] = line


def weights(conv_weight, w_value, w_out):
    layers = conv_weight.shape[0]
    small = pl.BlockSpec((64, 64), lambda i: (0, 0))
    big = pl.BlockSpec((256, 256), lambda i: (0, 0))
    return pl.pallas_call(
        weights_kernel,
        out_shape=[
            jax.ShapeDtypeStruct((layers, 3, 256, 384), bf16),
            jax.ShapeDtypeStruct((256, 256), bf16),
            jax.ShapeDtypeStruct((256, 256), bf16),
        ],
        grid=(layers,),
        in_specs=[pl.BlockSpec((1, 27, 64, 64), lambda i: (i, 0, 0, 0)), small, small],
        out_specs=[pl.BlockSpec((1, 3, 256, 384), lambda i: (i, 0, 0, 0)), big, big],
        scratch_shapes=[pltpu.VMEM((64, 64), f32)],
        compiler_params=pltpu.CompilerParams(
            dimension_semantics=("arbitrary",), vmem_limit_bytes=8 << 20
        ),
        cost_estimate=pl.CostEstimate(flops=10**6, bytes_accessed=8 << 20, transcendentals=0),
        name="weights",
    )(conv_weight.reshape(layers, 27, 64, 64), w_value, w_out)


def row_mask(mask):
    xi = lax.axis_index("frame") % 4
    x0, y0 = lax.axis_index("bx") * 8 - halo, lax.axis_index("by") * 128 + xi * 32 - halo
    y = lax.broadcasted_iota(jnp.int32, (stride, 128), 0) + y0
    y_ok = (y >= 0) & (y < 512)
    for x in range(16):
        line = jnp.where(y_ok & (x0 + x >= 0) & (x0 + x < 32), 1.0, 0.0)
        mask[stride * x : stride * x + stride, :] = line


def pair_rows(src, shift, lines, t, layer, band, bias):
    acc = None
    for b in range(3):
        at = [(stride * (i - shift + b - 1), stride * (j - shift + b - 1)) for i, j in lines]
        rows = [src[i:j, 128 * t : 128 * t + 256] for i, j in at]
        rows = rows[0] if len(rows) == 1 else jnp.concatenate(rows, axis=0)
        term = dot(rows, band[layer, b])
        acc = term if acc is None else acc + term
    n = acc.shape[0]
    h = acc[:, 128:256] + bias[layer : layer + 1, :]
    return h + pltpu.roll(acc[:, 0:128], 1, 0) + pltpu.roll(acc[:, 256:384], n - 1, 0)


def keep(h, dst, shift, lines, t, layer, mask):
    z0 = lax.axis_index("frame") // 4 * 4 - halo
    lane = lax.broadcasted_iota(jnp.int32, (1, 128), 1)
    z = z0 + layer + 1 + 2 * t + lane // 64
    z_ok = jnp.where((z >= 0) & (z < 16), 1.0, 0.0)
    at = 0
    for i, j in lines:
        n = stride * (j - i)
        ok = z_ok * mask[stride * i : stride * j, :]
        part = jnp.where(ok > 0, jnp.maximum(h[at : at + n], 0.0), 0.0)
        row = stride * (i - shift)
        dst[row : row + n, 128 * t : 128 * t + 128] = part.astype(bf16)
        at += n


def core_kernel(block, band, bias, out0, out1, out2, mask):
    row_mask(mask)
    src, shift = block, 4
    for layer, dst in enumerate((out0, out1, out2)):
        lines = [(5 + layer, 11 - layer)]
        for t in range(5 - layer):
            h = pair_rows(src, shift, lines, t, layer, band, bias)
            keep(h, dst, 5 + layer, lines, t, layer, mask)
        src, shift = dst, 5 + layer


def core(block, band, bias):
    widths = (640, 512, 384)
    return pl.pallas_call(
        core_kernel,
        out_shape=[
            jax.ShapeDtypeStruct((stride * (6 - 2 * i), w), bf16) for i, w in enumerate(widths)
        ],
        in_specs=[VM] * 3,
        out_specs=[VM] * 3,
        scratch_shapes=[pltpu.VMEM((16 * stride, 128), f32)],
        compiler_params=pltpu.CompilerParams(vmem_limit_bytes=8 << 20),
        cost_estimate=pl.CostEstimate(flops=10**9, bytes_accessed=10**6, transcendentals=0),
        name="core",
    )(block, band, bias)


def conv_kernel(block, core0, core1, core2, band, bias, out, buf0, buf1, mask):
    xi = lax.axis_index("frame") % 4
    row_mask(mask)
    src = block
    for layer, (dst, done) in enumerate(((buf0, core0), (buf1, core1), (buf0, core2))):
        width = done.shape[1]
        dst[stride * (5 + layer) : stride * (11 - layer), 0:width] = done[...]
        lines = [(1 + layer, 5 + layer), (11 - layer, 15 - layer)]
        for t in range(5 - layer):
            h = pair_rows(src, 0, lines, t, layer, band, bias)
            keep(h, dst, 0, lines, t, layer, mask)
        src = dst
    for t in range(2):
        h = pair_rows(src, 0, [(4, 12)], t, 3, band, bias)
        h = pltpu.roll(h, h.shape[0] - halo, 0)
        tiles = [h[stride * x : stride * x + 32] for x in range(8)]
        whole = jnp.concatenate(tiles, axis=0).T.astype(bf16)
        for i in range(2):
            out[(2 * t + i - xi) & 3] = whole[64 * i : 64 * i + 64]


def convolve(block, cores, band, bias):
    return pl.pallas_call(
        conv_kernel,
        out_shape=jax.ShapeDtypeStruct((4, 64, 256), bf16),
        in_specs=[VM] * 6,
        out_specs=VM,
        scratch_shapes=[
            pltpu.VMEM((16 * stride, 640), bf16),
            pltpu.VMEM((16 * stride, 512), bf16),
            pltpu.VMEM((16 * stride, 128), f32),
        ],
        compiler_params=pltpu.CompilerParams(vmem_limit_bytes=16 << 20),
        name="convolve",
    )(block, *cores, band, bias)


def place_kernel(own, high, far, low, out, rows):
    turn = 32 * (lax.axis_index("frame") % 4)
    parts = [r[...].astype(f32) for r in (own, high, far, low)]
    for x in range(8):
        line = jnp.concatenate([p[:, 32 * x : 32 * x + 32] for p in parts], axis=1)
        rows[pl.ds(x, 64, stride=8), :] = pltpu.roll(line, turn, 1)
    out[...] = rows[...].astype(bf16)


def place(own, high, far, low):
    return pl.pallas_call(
        place_kernel,
        out_shape=jax.ShapeDtypeStruct((512, 128), bf16),
        in_specs=[VM] * 4,
        out_specs=VM,
        scratch_shapes=[pltpu.VMEM((512, 128), f32)],
        compiler_params=pltpu.CompilerParams(vmem_limit_bytes=4 << 20),
        name="place",
    )(own, high, far, low)


def send(v, way, axis="frame"):
    return lax.ppermute(v, axis, way)


def only(inside, v):
    return jnp.where(inside, v, jnp.zeros_like(v))


def joined(features, voxel_embed, visible, w_query, w_key, w_value, w_out, conv_weight, conv_bias):
    around = range(4)
    x_by = lambda k: [(4 * z + x, 4 * z + (x + k) % 4) for z in around for x in around]
    up, down = x_by(1), x_by(3)
    z_up = [(i, (i + 4) % 16) for i in range(16)]
    z_down = [(j, i) for i, j in z_up]
    frames, planes, c = features.shape[:3]
    feat = features.reshape(frames, planes, c * 8, 128)
    embed = voxel_embed.reshape(planes, c * 8, 128)
    a0, a1, a2, a3 = attend(0, feat, embed, visible, w_query, w_key)
    from_low = send(a2, up)
    high_a = send(a3, down)
    b0, b1, b2, b3 = attend(1, feat, embed, visible, w_query, w_key)
    band, wide_v, wide_o = weights(conv_weight, w_value, w_out)
    from_high = send(b2, down)
    low_b = send(b1, up)
    low_a = send(merge([a1, from_low], [8])[0], up)
    high_b = send(merge([b3, from_high], [8])[0], down)
    z1, z2a, z2b = merge([a0, low_a, high_a], [4, 2, 2])
    from_low = send(z2a, z_up)
    from_high = send(z2b, z_down)
    low = send(lift(0, z1, from_low), z_up)
    z3, z0 = merge([b0, low_b, high_b], [4, 4])
    high = send(lift(2, z3, from_high), z_down)
    hidden = finish(z0, low, high, wide_v, wide_o).reshape(8, 32, 256)

    me = lax.axis_index("frame")
    zh, xi = me // 4, me % 4
    below = only(zh > 0, send(hidden, z_up))
    above = only(zh < 3, send(hidden, z_down))
    hidden = jnp.concatenate([below, hidden, above], axis=2)

    def where_is(z, chunk):
        return (4 * z + chunk % 4) * 4 + chunk // 4

    y_next = [(where_is(z, k), where_is(z, (k + 1) % 16)) for z in range(4) for k in range(16)]
    y_prev = [(j, i) for i, j in y_next]
    chunk = lax.axis_index("by") * 4 + xi
    left = only(chunk > 0, send(hidden[:, -halo:], y_next, ("frame", "by")))
    right = only(chunk < 15, send(hidden[:, :halo], y_prev, ("frame", "by")))
    first, second = (
        jnp.concatenate([left[i], hidden[i], right[i]], axis=1)
        for i in (slice(0, halo), slice(halo, None))
    )
    x_next = [(i, (i + 1) % 4) for i in range(4)]
    x_prev = [(j, i) for i, j in x_next]
    bx = lax.axis_index("bx")
    front = only(bx > 0, send(second, x_next, "bx"))
    back = only(bx < 3, send(first, x_prev, "bx"))
    bias = jnp.concatenate([conv_bias, conv_bias], axis=1)

    def lines(*parts):
        whole = jnp.concatenate(parts, axis=0)
        pad = jnp.zeros((whole.shape[0], stride - 32 - 2 * halo, 768), bf16)
        return jnp.concatenate([whole, pad], axis=1).reshape(-1, 768)

    cores = core(lines(first, second), band, bias)
    out = convolve(lines(front, first, second, back), cores, band, bias)
    low = send(out[1], up)
    high = send(out[3], down)
    far = send(out[2], x_by(2))
    return place(out[0], high, far, low).reshape(1, c, 8, 128)


def solution(mesh):
    return jax.shard_map(
        joined,
        mesh=mesh,
        in_specs=(
            P("frame", None, None, "bx", "by"),
            P(None, None, "bx", "by"),
            P("frame", None, "bx", "by"),
            P(),
            P(),
            P(),
            P(),
            P(),
            P(),
        ),
        out_specs=P("frame", None, "bx", "by"),
        check_vma=False,
    )
```

```python
import functools

import jax
import jax.numpy as jnp
from jax import lax
from jax.experimental import pallas as pl
from jax.experimental.pallas import tpu as pltpu
from jax.sharding import PartitionSpec as P


absent_score = -1e30
halo = 4
stride = 48
bf16, f32 = jnp.bfloat16, jnp.float32
VM = pl.BlockSpec(memory_space=pltpu.VMEM)


def chunk_of():
    x, odd = lax.axis_index("frame") % 4, lax.axis_index("by") % 2
    return x + odd * (3 - 2 * x)


def dot(a, b):
    return jnp.dot(a, b, preferred_element_type=f32)


def lane_blocks(v):
    lane = lax.broadcasted_iota(jnp.int32, (8, 128), 1)
    low = lane < 64
    even = (lane & 63) < 32
    t = [None] * 4
    for i in (0, 1):
        t[i] = jnp.where(low, v[i], pltpu.roll(v[i + 2], 64, 1))
        t[i + 2] = jnp.where(low, pltpu.roll(v[i], 64, 1), v[i + 2])
    o = [None] * 4
    for i in (0, 2):
        o[i] = jnp.where(even, t[i], pltpu.roll(t[i + 1], 32, 1))
        o[i + 1] = jnp.where(even, pltpu.roll(t[i], 96, 1), t[i + 1])
    return o


def three_terms(m):
    hi = m.astype(bf16).astype(f32)
    mid = (m - hi).astype(bf16).astype(f32)
    return hi, mid, m - hi - mid


def attend_kernel(half, feat_at, embed_at, seen_at, wq_at, wk_at, *refs):
    outs, feat, embed, seen, wq, wk, key0, key1, wide0, wide1, sems = refs[:4], *refs[4:]
    steps, frames, n = feat.shape[:3]
    zh = lax.axis_index("frame") // 4
    turn = (128 - 32 * chunk_of()) & 127

    def copies(s):
        block = 1 + 2 * half + s * n // 4
        z = pl.ds(((block + zh) & 3) * 4 + s * n % 4, n)
        return [
            pltpu.make_async_copy(embed_at.at[z], embed.at[s], sems.at[s, 0]),
            pltpu.make_async_copy(feat_at.at[:, z], feat.at[s], sems.at[s, 1]),
            pltpu.make_async_copy(seen_at.at[:, z], seen.at[s], sems.at[s, 2]),
        ]

    loads = [copies(s) for s in range(steps)]
    small = [
        pltpu.make_async_copy(wq_at, wq, sems.at[steps, 0]),
        pltpu.make_async_copy(wk_at, wk, sems.at[steps, 1]),
    ]
    for c in [loads[0][0], *small, *loads[0][1:], *sum(loads[1:], [])]:
        c.start()
    for c in small:
        c.wait()

    def keys(s):
        key = (key0, key1)[s % 2]
        loads[s][0].wait()
        for p in range(n):
            key[p] = embed[s, p].astype(f32)
        cols = [key[p, pl.ds(i, 64, stride=8), :] for p in range(n) for i in range(8)]
        wide = jnp.concatenate(cols, axis=1).astype(bf16)
        q = lax.dot_general(wq[...], wide, (((0,), (0,)), ((), ())), preferred_element_type=f32)
        qk = dot(wk[...], q.astype(bf16))
        for p in range(n):
            for i in range(8):
                at = (8 * p + i) * 128
                key[p, pl.ds(i, 64, stride=8), :] = qk[:, at : at + 128]

    def plane(s, p):
        key, wide = (key0, key1)[s % 2], (wide0, wide1)[p % 2]
        sums = [jnp.zeros((8, 128), f32) for _ in range(frames)]
        for g in range(16):
            rows = slice(32 * g, 32 * g + 32)
            line = key[p, rows, :]
            for f in range(frames):
                value = feat[s, f, p, rows, :].astype(f32)
                wide[f, rows, :] = value
                sums[f] = sums[f] + jnp.sum((line * value).reshape(4, 8, 128), axis=0)
        sums = [v * 0.125 for v in sums]
        ok = [seen[s, f, p] > 0 for f in range(frames)]
        m = jnp.full((8, 128), absent_score, f32)
        for f in range(frames):
            m = jnp.maximum(m, jnp.where(ok[f], sums[f], absent_score))
        e = [jnp.where(ok[f], jnp.exp(sums[f] - m), 0.0) for f in range(frames)]
        total = e[0]
        for f in range(1, frames):
            total = total + e[f]

        def put(g, tiles):
            tiles = [pltpu.roll(t, turn, 1) for t in tiles]
            for out, tile in zip(outs, lane_blocks(tiles)):
                out[s * n + p, 8 * g : 8 * g + 8, :] = tile.astype(bf16)

        for g in range(16):
            rows = slice(32 * g, 32 * g + 32)
            acc = None
            for f in range(frames):
                term = e[f][None] * wide[f, rows, :].reshape(4, 8, 128)
                acc = term if acc is None else acc + term
            put(g, [acc[i] for i in range(4)])
        put(16, [*three_terms(m), total])

    keys(0)
    for s in range(steps):
        loads[s][1].wait()
        loads[s][2].wait()
        if s + 1 < steps:
            keys(s + 1)
        for p in range(n):
            plane(s, p)


def attend(half, feat, embed, visible, w_query, w_key):
    frames, planes, rows = feat.shape[:3]
    c = w_key.shape[0]
    n = 2
    count = planes // 2
    steps = count // n
    hbm = pl.BlockSpec(memory_space=pltpu.HBM)
    return pl.pallas_call(
        functools.partial(attend_kernel, half),
        out_shape=[jax.ShapeDtypeStruct((count, 136, 128), bf16)] * 4,
        in_specs=[hbm] * 5,
        out_specs=[VM] * 4,
        scratch_shapes=[
            pltpu.VMEM((steps, frames, n, rows, 128), bf16),
            pltpu.VMEM((steps, n, rows, 128), bf16),
            pltpu.VMEM((steps, frames, n, 8, 128), jnp.int32),
            pltpu.VMEM((c, c), bf16),
            pltpu.VMEM((c, c), bf16),
            pltpu.VMEM((n, rows, 128), f32),
            pltpu.VMEM((n, rows, 128), f32),
            pltpu.VMEM((frames, rows, 128), f32),
            pltpu.VMEM((frames, rows, 128), f32),
            pltpu.SemaphoreType.DMA((steps + 1, 3)),
        ],
        compiler_params=pltpu.CompilerParams(vmem_limit_bytes=16 << 20),
        cost_estimate=pl.CostEstimate(flops=10**8, bytes_accessed=12 << 20, transcendentals=0),
        name="attend",
    )(*[pltpu.with_memory_space_constraint(v, pltpu.HBM) for v in (feat, embed, visible, w_query, w_key)])


def spread(v):
    u = v + pltpu.roll(v, 64, 1)
    return u + pltpu.roll(u, 32, 1)


def merged_plane(parts):
    lane = lax.broadcasted_iota(jnp.int32, (8, 128), 1)
    tail = lane >= 96
    stats = [r[p, 128:136, :].astype(f32) for r, p in parts]
    ms = [spread(jnp.where(tail, 0.0, s)) for s in stats]
    ls = [spread(jnp.where(tail, s, 0.0)) for s in stats]
    m = functools.reduce(jnp.maximum, ms)
    ws = [jnp.exp(v - m) for v in ms]
    total = sum(w * v for w, v in zip(ws, ls))
    return ws, total, m


def weighted_rows(parts, ws):
    acc = None
    for (r, p), w in zip(parts, ws):
        term = r[p, 0:128, :].astype(f32).reshape(16, 8, 128) * w[None]
        acc = term if acc is None else acc + term
    return acc.reshape(128, 128)


def merge_plane(out, i, parts):
    lane = lax.broadcasted_iota(jnp.int32, (8, 128), 1)
    ws, total, m = merged_plane(parts)
    out[i, 0:128, :] = weighted_rows(parts, ws).astype(bf16)
    hi, mid, low = three_terms(m)
    packed = jnp.where(
        lane < 32, hi, jnp.where(lane < 64, mid, jnp.where(lane >= 96, total, low))
    )
    out[i, 128:136, :] = packed.astype(bf16)


def merge_kernel(n, sizes, *refs):
    ins, outs = refs[:n], refs[n:]
    at = 0
    for out, size in zip(outs, sizes):
        for i in range(size):
            merge_plane(out, i, [(r, at) for r in ins])
            at += 1


def merge(parts, sizes):
    n = parts[0].shape[0]
    return pl.pallas_call(
        functools.partial(merge_kernel, len(parts), sizes),
        out_shape=[jax.ShapeDtypeStruct((s, 136, 128), bf16) for s in sizes],
        in_specs=[VM] * len(parts),
        out_specs=[VM] * len(sizes),
        compiler_params=pltpu.CompilerParams(vmem_limit_bytes=6 << 20),
        cost_estimate=pl.CostEstimate(flops=n * 10**5, bytes_accessed=n * 10**5, transcendentals=0),
        name="merge",
    )(*parts)


def lift_kernel(at, slot, came, out):
    other = 2 - at
    out[other : other + 2] = slot[other : other + 2]
    for i in range(2):
        merge_plane(out, at + i, [(slot, at + i), (came, i)])


def lift(at, slot, came):
    return pl.pallas_call(
        functools.partial(lift_kernel, at),
        out_shape=jax.ShapeDtypeStruct(slot.shape, bf16),
        in_specs=[VM] * 2,
        out_specs=VM,
        compiler_params=pltpu.CompilerParams(vmem_limit_bytes=4 << 20),
        cost_estimate=pl.CostEstimate(flops=10**5, bytes_accessed=10**5, transcendentals=0),
        name="lift",
    )(slot, came)


def finish_kernel(own, low, high, wv, wo, out, rows):
    for p in range(4):
        parts = [(own, p), (low, p), (high, p)]
        ws, total, _ = merged_plane(parts)
        inv = 1.0 / total
        rows[128 * p : 128 * p + 128, :] = weighted_rows(parts, [w * inv for w in ws])
    lines = []
    for x in range(8):
        t = rows[pl.ds(x, 64, stride=8), :].T
        lines.append(jnp.concatenate([t[32 * i : 32 * i + 32] for i in range(4)], axis=1))
    mixed = jnp.concatenate(lines, axis=0).astype(bf16)
    attended = dot(mixed, wv[...]).astype(bf16)
    out[...] = dot(attended, wo[...]).astype(bf16)


def finish(own, low, high, wv, wo):
    return pl.pallas_call(
        finish_kernel,
        out_shape=jax.ShapeDtypeStruct((256, 256), bf16),
        in_specs=[VM] * 5,
        out_specs=VM,
        scratch_shapes=[pltpu.VMEM((512, 128), f32)],
        compiler_params=pltpu.CompilerParams(vmem_limit_bytes=6 << 20),
        name="finish",
    )(own, low, high, wv, wo)


def weights_kernel(w, wv, wo, band, wide_v, wide_o, tmp):
    zero = jnp.zeros((64, 64), bf16)
    for tap in range(9):
        a = [w[0, 9 * i + tap] for i in range(3)]
        left = jnp.concatenate([a[0], a[1], a[2], zero], axis=0)
        right = jnp.concatenate([zero, a[0], a[1], a[2]], axis=0)
        e = tap % 3
        band[0, tap // 3, :, 128 * e : 128 * e + 128] = jnp.concatenate([left, right], axis=1)

    @pl.when(pl.program_id(0) == 0)
    def _():
        tmp[...] = wv[...].astype(f32)
        blank = jnp.zeros((16, 64), f32)
        for i in range(4):
            piece = tmp[pl.ds(i, 16, stride=4), :]
            for p in range(4):
                line = jnp.concatenate([piece if j == p else blank for j in range(4)], axis=1)
                at = 64 * i + 16 * p
                wide_v[at : at + 16, :] = line.astype(bf16)
        for p in range(4):
            line = jnp.concatenate([wo[...] if j == p else zero for j in range(4)], axis=1)
            wide_o[64 * p : 64 * p + 64, :] = line


def weights(conv_weight, w_value, w_out):
    layers = conv_weight.shape[0]
    small = pl.BlockSpec((64, 64), lambda i: (0, 0))
    big = pl.BlockSpec((256, 256), lambda i: (0, 0))
    return pl.pallas_call(
        weights_kernel,
        out_shape=[
            jax.ShapeDtypeStruct((layers, 3, 256, 384), bf16),
            jax.ShapeDtypeStruct((256, 256), bf16),
            jax.ShapeDtypeStruct((256, 256), bf16),
        ],
        grid=(layers,),
        in_specs=[pl.BlockSpec((1, 27, 64, 64), lambda i: (i, 0, 0, 0)), small, small],
        out_specs=[pl.BlockSpec((1, 3, 256, 384), lambda i: (i, 0, 0, 0)), big, big],
        scratch_shapes=[pltpu.VMEM((64, 64), f32)],
        compiler_params=pltpu.CompilerParams(
            dimension_semantics=("arbitrary",), vmem_limit_bytes=8 << 20
        ),
        cost_estimate=pl.CostEstimate(flops=10**6, bytes_accessed=8 << 20, transcendentals=0),
        name="weights",
    )(conv_weight.reshape(layers, 27, 64, 64), w_value, w_out)


def row_mask(mask):
    x0 = lax.axis_index("bx") * 8 - halo
    y0 = lax.axis_index("by") * 128 + chunk_of() * 32 - halo
    y = lax.broadcasted_iota(jnp.int32, (stride, 128), 0) + y0
    y_ok = (y >= 0) & (y < 512)
    for x in range(16):
        line = jnp.where(y_ok & (x0 + x >= 0) & (x0 + x < 32), 1.0, 0.0)
        mask[stride * x : stride * x + stride, :] = line


def pair_rows(src, shift, lines, t, layer, band, bias):
    acc = None
    for b in range(3):
        at = [(stride * (i - shift + b - 1), stride * (j - shift + b - 1)) for i, j in lines]
        rows = [src[i:j, 128 * t : 128 * t + 256] for i, j in at]
        rows = rows[0] if len(rows) == 1 else jnp.concatenate(rows, axis=0)
        term = dot(rows, band[layer, b])
        acc = term if acc is None else acc + term
    n = acc.shape[0]
    h = acc[:, 128:256] + bias[layer : layer + 1, :]
    return h + pltpu.roll(acc[:, 0:128], 1, 0) + pltpu.roll(acc[:, 256:384], n - 1, 0)


def keep(h, dst, shift, lines, t, layer, mask):
    z0 = lax.axis_index("frame") // 4 * 4 - halo
    lane = lax.broadcasted_iota(jnp.int32, (1, 128), 1)
    z = z0 + layer + 1 + 2 * t + lane // 64
    z_ok = jnp.where((z >= 0) & (z < 16), 1.0, 0.0)
    at = 0
    for i, j in lines:
        n = stride * (j - i)
        ok = z_ok * mask[stride * i : stride * j, :]
        part = jnp.where(ok > 0, jnp.maximum(h[at : at + n], 0.0), 0.0)
        row = stride * (i - shift)
        dst[row : row + n, 128 * t : 128 * t + 128] = part.astype(bf16)
        at += n


def core_kernel(block, band, bias, out0, out1, out2, mask):
    row_mask(mask)
    src, shift = block, 4
    for layer, dst in enumerate((out0, out1, out2)):
        lines = [(5 + layer, 11 - layer)]
        for t in range(5 - layer):
            h = pair_rows(src, shift, lines, t, layer, band, bias)
            keep(h, dst, 5 + layer, lines, t, layer, mask)
        src, shift = dst, 5 + layer


def core(block, band, bias):
    widths = (640, 512, 384)
    return pl.pallas_call(
        core_kernel,
        out_shape=[
            jax.ShapeDtypeStruct((stride * (6 - 2 * i), w), bf16) for i, w in enumerate(widths)
        ],
        in_specs=[VM] * 3,
        out_specs=[VM] * 3,
        scratch_shapes=[pltpu.VMEM((16 * stride, 128), f32)],
        compiler_params=pltpu.CompilerParams(vmem_limit_bytes=8 << 20),
        cost_estimate=pl.CostEstimate(flops=10**9, bytes_accessed=10**6, transcendentals=0),
        name="core",
    )(block, band, bias)


def conv_kernel(block, core0, core1, core2, band, bias, out, buf0, buf1, mask):
    mine, odd = chunk_of(), lax.axis_index("by") % 2
    row_mask(mask)
    src = block
    for layer, (dst, done) in enumerate(((buf0, core0), (buf1, core1), (buf0, core2))):
        width = done.shape[1]
        dst[stride * (5 + layer) : stride * (11 - layer), 0:width] = done[...]
        lines = [(1 + layer, 5 + layer), (11 - layer, 15 - layer)]
        for t in range(5 - layer):
            h = pair_rows(src, 0, lines, t, layer, band, bias)
            keep(h, dst, 0, lines, t, layer, mask)
        src = dst
    for t in range(2):
        h = pair_rows(src, 0, [(4, 12)], t, 3, band, bias)
        h = pltpu.roll(h, h.shape[0] - halo, 0)
        tiles = [h[stride * x : stride * x + 32] for x in range(8)]
        whole = jnp.concatenate(tiles, axis=0).T.astype(bf16)
        for i in range(2):
            goal = 2 * t + i
            goal = goal + odd * (3 - 2 * goal)
            out[(goal - mine) & 3] = whole[64 * i : 64 * i + 64]


def convolve(block, cores, band, bias):
    return pl.pallas_call(
        conv_kernel,
        out_shape=jax.ShapeDtypeStruct((4, 64, 256), bf16),
        in_specs=[VM] * 6,
        out_specs=VM,
        scratch_shapes=[
            pltpu.VMEM((16 * stride, 640), bf16),
            pltpu.VMEM((16 * stride, 512), bf16),
            pltpu.VMEM((16 * stride, 128), f32),
        ],
        compiler_params=pltpu.CompilerParams(vmem_limit_bytes=16 << 20),
        name="convolve",
    )(block, *cores, band, bias)


def place_kernel(own, high, far, low, out, rows):
    turn = 32 * chunk_of()
    parts = [r[...].astype(f32) for r in (own, high, far, low)]
    for x in range(8):
        line = jnp.concatenate([p[:, 32 * x : 32 * x + 32] for p in parts], axis=1)
        rows[pl.ds(x, 64, stride=8), :] = pltpu.roll(line, turn, 1)
    out[...] = rows[...].astype(bf16)


def place(own, high, far, low):
    return pl.pallas_call(
        place_kernel,
        out_shape=jax.ShapeDtypeStruct((512, 128), bf16),
        in_specs=[VM] * 4,
        out_specs=VM,
        scratch_shapes=[pltpu.VMEM((512, 128), f32)],
        compiler_params=pltpu.CompilerParams(vmem_limit_bytes=4 << 20),
        name="place",
    )(own, high, far, low)


def send(v, way, axis=("frame", "by")):
    return lax.ppermute(v, axis, way)


def only(inside, v):
    return jnp.where(inside, v, jnp.zeros_like(v))


def joined(features, voxel_embed, visible, w_query, w_key, w_value, w_out, conv_weight, conv_bias):
    around = range(4)

    def where_is(z, chunk):
        brick, k = chunk // 4, chunk % 4
        return (4 * z + (3 - k if brick % 2 else k)) * 4 + brick

    def x_by(r):
        bases = [(z, 4 * brick, k) for z in around for brick in around for k in around]
        return [(where_is(z, b + k), where_is(z, b + (k + r) % 4)) for z, b, k in bases]

    up, down = x_by(1), x_by(3)
    z_up = [(i, (i + 4) % 16) for i in range(16)]
    z_down = [(j, i) for i, j in z_up]
    frames, planes, c = features.shape[:3]
    feat = features.reshape(frames, planes, c * 8, 128)
    embed = voxel_embed.reshape(planes, c * 8, 128)
    a0, a1, a2, a3 = attend(0, feat, embed, visible, w_query, w_key)
    from_low = send(a2, up)
    high_a = send(a3, down)
    b0, b1, b2, b3 = attend(1, feat, embed, visible, w_query, w_key)
    band, wide_v, wide_o = weights(conv_weight, w_value, w_out)
    from_high = send(b2, down)
    low_b = send(b1, up)
    low_a = send(merge([a1, from_low], [8])[0], up)
    high_b = send(merge([b3, from_high], [8])[0], down)
    z1, z2a, z2b = merge([a0, low_a, high_a], [4, 2, 2])
    from_low = send(z2a, z_up, "frame")
    from_high = send(z2b, z_down, "frame")
    low = send(lift(0, z1, from_low), z_up, "frame")
    z3, z0 = merge([b0, low_b, high_b], [4, 4])
    high = send(lift(2, z3, from_high), z_down, "frame")
    hidden = finish(z0, low, high, wide_v, wide_o).reshape(8, 32, 256)

    me = lax.axis_index("frame")
    zh = me // 4
    below = only(zh > 0, send(hidden, z_up, "frame"))
    above = only(zh < 3, send(hidden, z_down, "frame"))
    hidden = jnp.concatenate([below, hidden, above], axis=2)

    y_next = [(where_is(z, k), where_is(z, (k + 1) % 16)) for z in range(4) for k in range(16)]
    y_prev = [(j, i) for i, j in y_next]
    chunk = lax.axis_index("by") * 4 + chunk_of()
    left = only(chunk > 0, send(hidden[:, -halo:], y_next))
    right = only(chunk < 15, send(hidden[:, :halo], y_prev))
    first, second = (
        jnp.concatenate([left[i], hidden[i], right[i]], axis=1)
        for i in (slice(0, halo), slice(halo, None))
    )
    x_next = [(i, (i + 1) % 4) for i in range(4)]
    x_prev = [(j, i) for i, j in x_next]
    bx = lax.axis_index("bx")
    front = only(bx > 0, send(second, x_next, "bx"))
    back = only(bx < 3, send(first, x_prev, "bx"))
    bias = jnp.concatenate([conv_bias, conv_bias], axis=1)

    def lines(*parts):
        whole = jnp.concatenate(parts, axis=0)
        pad = jnp.zeros((whole.shape[0], stride - 32 - 2 * halo, 768), bf16)
        return jnp.concatenate([whole, pad], axis=1).reshape(-1, 768)

    cores = core(lines(first, second), band, bias)
    out = convolve(lines(front, first, second, back), cores, band, bias)
    low = send(out[1], up)
    high = send(out[3], down)
    far = send(out[2], x_by(2))
    return place(out[0], high, far, low).reshape(1, c, 8, 128)


def solution(mesh):
    return jax.shard_map(
        joined,
        mesh=mesh,
        in_specs=(
            P("frame", None, None, "bx", "by"),
            P(None, None, "bx", "by"),
            P("frame", None, "bx", "by"),
            P(),
            P(),
            P(),
            P(),
            P(),
            P(),
        ),
        out_specs=P("frame", None, "bx", "by"),
        check_vma=False,
    )
```

```python
import functools

import jax
import jax.numpy as jnp
from jax import lax
from jax.experimental import pallas as pl
from jax.experimental.pallas import tpu as pltpu
from jax.sharding import PartitionSpec as P


absent_score = -1e30
halo = 4
stride = 48
bf16, f32 = jnp.bfloat16, jnp.float32
VM = pl.BlockSpec(memory_space=pltpu.VMEM)


def dot(a, b):
    return jnp.dot(a, b, preferred_element_type=f32)


def lane_blocks(v):
    lane = lax.broadcasted_iota(jnp.int32, (8, 128), 1)
    low = lane < 64
    even = (lane & 63) < 32
    t = [None] * 4
    for i in (0, 1):
        t[i] = jnp.where(low, v[i], pltpu.roll(v[i + 2], 64, 1))
        t[i + 2] = jnp.where(low, pltpu.roll(v[i], 64, 1), v[i + 2])
    o = [None] * 4
    for i in (0, 2):
        o[i] = jnp.where(even, t[i], pltpu.roll(t[i + 1], 32, 1))
        o[i + 1] = jnp.where(even, pltpu.roll(t[i], 96, 1), t[i + 1])
    return o


def three_terms(m):
    hi = m.astype(bf16).astype(f32)
    mid = (m - hi).astype(bf16).astype(f32)
    return hi, mid, m - hi - mid


def attend_kernel(ahead, feat_at, embed_at, seen_at, wq_at, wk_at, *refs):
    outs, feat, embed, seen, wq, wk, key0, key1, wide0, wide1, sems = refs[:4], *refs[4:]
    steps, frames, n = feat.shape[:3]
    me = lax.axis_index("frame")
    zh, xi = me // 4, me % 4
    turn = (128 - 32 * zh) & 127

    def copies(s):
        z = pl.ds(((xi + ahead[s // 2]) & 3) * 4 + s % 2 * n, n)
        return [
            pltpu.make_async_copy(embed_at.at[z], embed.at[s], sems.at[s, 0]),
            pltpu.make_async_copy(feat_at.at[:, z], feat.at[s], sems.at[s, 1]),
            pltpu.make_async_copy(seen_at.at[:, z], seen.at[s], sems.at[s, 2]),
        ]

    loads = [copies(s) for s in range(steps)]
    small = [
        pltpu.make_async_copy(wq_at, wq, sems.at[steps, 0]),
        pltpu.make_async_copy(wk_at, wk, sems.at[steps, 1]),
    ]
    for c in [loads[0][0], *small, *loads[0][1:], *sum(loads[1:], [])]:
        c.start()
    for c in small:
        c.wait()

    def keys(s):
        key = (key0, key1)[s % 2]
        loads[s][0].wait()
        for p in range(n):
            key[p] = embed[s, p].astype(f32)
        cols = [key[p, pl.ds(i, 64, stride=8), :] for p in range(n) for i in range(8)]
        wide = jnp.concatenate(cols, axis=1).astype(bf16)
        q = lax.dot_general(wq[...], wide, (((0,), (0,)), ((), ())), preferred_element_type=f32)
        qk = dot(wk[...], q.astype(bf16))
        for p in range(n):
            for i in range(8):
                at = (8 * p + i) * 128
                key[p, pl.ds(i, 64, stride=8), :] = qk[:, at : at + 128]

    def plane(s, p):
        key, wide = (key0, key1)[s % 2], (wide0, wide1)[p % 2]
        sums = [jnp.zeros((8, 128), f32) for _ in range(frames)]
        for g in range(16):
            rows = slice(32 * g, 32 * g + 32)
            line = key[p, rows, :]
            for f in range(frames):
                value = feat[s, f, p, rows, :].astype(f32)
                wide[f, rows, :] = value
                sums[f] = sums[f] + jnp.sum((line * value).reshape(4, 8, 128), axis=0)
        sums = [v * 0.125 for v in sums]
        ok = [seen[s, f, p] > 0 for f in range(frames)]
        m = jnp.full((8, 128), absent_score, f32)
        for f in range(frames):
            m = jnp.maximum(m, jnp.where(ok[f], sums[f], absent_score))
        e = [jnp.where(ok[f], jnp.exp(sums[f] - m), 0.0) for f in range(frames)]
        total = e[0]
        for f in range(1, frames):
            total = total + e[f]

        def put(g, tiles):
            tiles = [pltpu.roll(t, turn, 1) for t in tiles]
            for q, tile in enumerate(lane_blocks(tiles)):
                unit = (q + 1) % 2 * 4 + s % 2 * n + p
                out = outs[s // 2 * 2 + (0 if q in (1, 2) else 1)]
                out[unit, 8 * g : 8 * g + 8, :] = tile.astype(bf16)

        for g in range(16):
            rows = slice(32 * g, 32 * g + 32)
            acc = None
            for f in range(frames):
                term = e[f][None] * wide[f, rows, :].reshape(4, 8, 128)
                acc = term if acc is None else acc + term
            put(g, [acc[i] for i in range(4)])
        put(16, [*three_terms(m), total])

    keys(0)
    for s in range(steps):
        loads[s][1].wait()
        loads[s][2].wait()
        if s + 1 < steps:
            keys(s + 1)
        for p in range(n):
            plane(s, p)


def attend(ahead, feat, embed, visible, w_query, w_key):
    frames, planes, rows = feat.shape[:3]
    c = w_key.shape[0]
    n = 2
    count = planes // 2
    steps = count // n
    hbm = pl.BlockSpec(memory_space=pltpu.HBM)
    return pl.pallas_call(
        functools.partial(attend_kernel, ahead),
        out_shape=[jax.ShapeDtypeStruct((count, 136, 128), bf16)] * 4,
        in_specs=[hbm] * 5,
        out_specs=[VM] * 4,
        scratch_shapes=[
            pltpu.VMEM((steps, frames, n, rows, 128), bf16),
            pltpu.VMEM((steps, n, rows, 128), bf16),
            pltpu.VMEM((steps, frames, n, 8, 128), jnp.int32),
            pltpu.VMEM((c, c), bf16),
            pltpu.VMEM((c, c), bf16),
            pltpu.VMEM((n, rows, 128), f32),
            pltpu.VMEM((n, rows, 128), f32),
            pltpu.VMEM((frames, rows, 128), f32),
            pltpu.VMEM((frames, rows, 128), f32),
            pltpu.SemaphoreType.DMA((steps + 1, 3)),
        ],
        compiler_params=pltpu.CompilerParams(vmem_limit_bytes=16 << 20),
        cost_estimate=pl.CostEstimate(flops=10**8, bytes_accessed=12 << 20, transcendentals=0),
        name="attend",
    )(*[pltpu.with_memory_space_constraint(v, pltpu.HBM) for v in (feat, embed, visible, w_query, w_key)])


def spread(v):
    u = v + pltpu.roll(v, 64, 1)
    return u + pltpu.roll(u, 32, 1)


def merged_plane(parts):
    lane = lax.broadcasted_iota(jnp.int32, (8, 128), 1)
    tail = lane >= 96
    stats = [r[p, 128:136, :].astype(f32) for r, p in parts]
    ms = [spread(jnp.where(tail, 0.0, s)) for s in stats]
    ls = [spread(jnp.where(tail, s, 0.0)) for s in stats]
    m = functools.reduce(jnp.maximum, ms)
    ws = [jnp.exp(v - m) for v in ms]
    total = sum(w * v for w, v in zip(ws, ls))
    return ws, total, m


def weighted_rows(parts, ws):
    acc = None
    for (r, p), w in zip(parts, ws):
        term = r[p, 0:128, :].astype(f32).reshape(16, 8, 128) * w[None]
        acc = term if acc is None else acc + term
    return acc.reshape(128, 128)


def merge_plane(out, i, parts):
    lane = lax.broadcasted_iota(jnp.int32, (8, 128), 1)
    ws, total, m = merged_plane(parts)
    out[i, 0:128, :] = weighted_rows(parts, ws).astype(bf16)
    hi, mid, low = three_terms(m)
    packed = jnp.where(
        lane < 32, hi, jnp.where(lane < 64, mid, jnp.where(lane >= 96, total, low))
    )
    out[i, 128:136, :] = packed.astype(bf16)


def merge_kernel(n, sizes, *refs):
    ins, outs = refs[:n], refs[n:]
    at = 0
    for out, size in zip(outs, sizes):
        for i in range(size):
            merge_plane(out, i, [(r, at) for r in ins])
            at += 1


def merge(parts, sizes):
    n = parts[0].shape[0]
    return pl.pallas_call(
        functools.partial(merge_kernel, len(parts), sizes),
        out_shape=[jax.ShapeDtypeStruct((s, 136, 128), bf16) for s in sizes],
        in_specs=[VM] * len(parts),
        out_specs=[VM] * len(sizes),
        compiler_params=pltpu.CompilerParams(vmem_limit_bytes=6 << 20),
        cost_estimate=pl.CostEstimate(flops=n * 10**5, bytes_accessed=n * 10**5, transcendentals=0),
        name="merge",
    )(*parts)


def lift_kernel(at, slot, came, out):
    other = 2 - at
    out[other : other + 2] = slot[other : other + 2]
    for i in range(2):
        merge_plane(out, at + i, [(slot, at + i), (came, i)])


def lift(at, slot, came):
    return pl.pallas_call(
        functools.partial(lift_kernel, at),
        out_shape=jax.ShapeDtypeStruct(slot.shape, bf16),
        in_specs=[VM] * 2,
        out_specs=VM,
        compiler_params=pltpu.CompilerParams(vmem_limit_bytes=4 << 20),
        cost_estimate=pl.CostEstimate(flops=10**5, bytes_accessed=10**5, transcendentals=0),
        name="lift",
    )(slot, came)


def finish_kernel(own, low, high, wv, wo, out, rows):
    for p in range(4):
        parts = [(own, p), (low, p), (high, p)]
        ws, total, _ = merged_plane(parts)
        inv = 1.0 / total
        rows[128 * p : 128 * p + 128, :] = weighted_rows(parts, [w * inv for w in ws])
    lines = []
    for x in range(8):
        t = rows[pl.ds(x, 64, stride=8), :].T
        lines.append(jnp.concatenate([t[32 * i : 32 * i + 32] for i in range(4)], axis=1))
    mixed = jnp.concatenate(lines, axis=0).astype(bf16)
    attended = dot(mixed, wv[...]).astype(bf16)
    out[...] = dot(attended, wo[...]).astype(bf16)


def finish(own, low, high, wv, wo):
    return pl.pallas_call(
        finish_kernel,
        out_shape=jax.ShapeDtypeStruct((256, 256), bf16),
        in_specs=[VM] * 5,
        out_specs=VM,
        scratch_shapes=[pltpu.VMEM((512, 128), f32)],
        compiler_params=pltpu.CompilerParams(vmem_limit_bytes=6 << 20),
        name="finish",
    )(own, low, high, wv, wo)


def weights_kernel(w, wv, wo, band, wide_v, wide_o, tmp):
    zero = jnp.zeros((64, 64), bf16)
    for tap in range(9):
        a = [w[0, 9 * i + tap] for i in range(3)]
        left = jnp.concatenate([a[0], a[1], a[2], zero], axis=0)
        right = jnp.concatenate([zero, a[0], a[1], a[2]], axis=0)
        e = tap % 3
        band[0, tap // 3, :, 128 * e : 128 * e + 128] = jnp.concatenate([left, right], axis=1)

    @pl.when(pl.program_id(0) == 0)
    def _():
        tmp[...] = wv[...].astype(f32)
        blank = jnp.zeros((16, 64), f32)
        for i in range(4):
            piece = tmp[pl.ds(i, 16, stride=4), :]
            for p in range(4):
                line = jnp.concatenate([piece if j == p else blank for j in range(4)], axis=1)
                at = 64 * i + 16 * p
                wide_v[at : at + 16, :] = line.astype(bf16)
        for p in range(4):
            line = jnp.concatenate([wo[...] if j == p else zero for j in range(4)], axis=1)
            wide_o[64 * p : 64 * p + 64, :] = line


def weights(conv_weight, w_value, w_out):
    layers = conv_weight.shape[0]
    small = pl.BlockSpec((64, 64), lambda i: (0, 0))
    big = pl.BlockSpec((256, 256), lambda i: (0, 0))
    return pl.pallas_call(
        weights_kernel,
        out_shape=[
            jax.ShapeDtypeStruct((layers, 3, 256, 384), bf16),
            jax.ShapeDtypeStruct((256, 256), bf16),
            jax.ShapeDtypeStruct((256, 256), bf16),
        ],
        grid=(layers,),
        in_specs=[pl.BlockSpec((1, 27, 64, 64), lambda i: (i, 0, 0, 0)), small, small],
        out_specs=[pl.BlockSpec((1, 3, 256, 384), lambda i: (i, 0, 0, 0)), big, big],
        scratch_shapes=[pltpu.VMEM((64, 64), f32)],
        compiler_params=pltpu.CompilerParams(
            dimension_semantics=("arbitrary",), vmem_limit_bytes=8 << 20
        ),
        cost_estimate=pl.CostEstimate(flops=10**6, bytes_accessed=8 << 20, transcendentals=0),
        name="weights",
    )(conv_weight.reshape(layers, 27, 64, 64), w_value, w_out)


def row_mask(mask):
    zh = lax.axis_index("frame") // 4
    x0, y0 = lax.axis_index("bx") * 8 - halo, lax.axis_index("by") * 128 + zh * 32 - halo
    y = lax.broadcasted_iota(jnp.int32, (stride, 128), 0) + y0
    y_ok = (y >= 0) & (y < 512)
    for x in range(16):
        line = jnp.where(y_ok & (x0 + x >= 0) & (x0 + x < 32), 1.0, 0.0)
        mask[stride * x : stride * x + stride, :] = line


def pair_rows(src, shift, lines, t, layer, band, bias):
    acc = None
    for b in range(3):
        at = [(stride * (i - shift + b - 1), stride * (j - shift + b - 1)) for i, j in lines]
        rows = [src[i:j, 128 * t : 128 * t + 256] for i, j in at]
        rows = rows[0] if len(rows) == 1 else jnp.concatenate(rows, axis=0)
        term = dot(rows, band[layer, b])
        acc = term if acc is None else acc + term
    n = acc.shape[0]
    h = acc[:, 128:256] + bias[layer : layer + 1, :]
    return h + pltpu.roll(acc[:, 0:128], 1, 0) + pltpu.roll(acc[:, 256:384], n - 1, 0)


def keep(h, dst, shift, lines, t, layer, mask):
    z0 = lax.axis_index("frame") % 4 * 4 - halo
    lane = lax.broadcasted_iota(jnp.int32, (1, 128), 1)
    z = z0 + layer + 1 + 2 * t + lane // 64
    z_ok = jnp.where((z >= 0) & (z < 16), 1.0, 0.0)
    at = 0
    for i, j in lines:
        n = stride * (j - i)
        ok = z_ok * mask[stride * i : stride * j, :]
        part = jnp.where(ok > 0, jnp.maximum(h[at : at + n], 0.0), 0.0)
        row = stride * (i - shift)
        dst[row : row + n, 128 * t : 128 * t + 128] = part.astype(bf16)
        at += n


def core_kernel(block, band, bias, out0, out1, out2, mask):
    row_mask(mask)
    src, shift = block, 4
    for layer, dst in enumerate((out0, out1, out2)):
        lines = [(5 + layer, 11 - layer)]
        for t in range(5 - layer):
            h = pair_rows(src, shift, lines, t, layer, band, bias)
            keep(h, dst, 5 + layer, lines, t, layer, mask)
        src, shift = dst, 5 + layer


def core(block, band, bias):
    widths = (640, 512, 384)
    return pl.pallas_call(
        core_kernel,
        out_shape=[
            jax.ShapeDtypeStruct((stride * (6 - 2 * i), w), bf16) for i, w in enumerate(widths)
        ],
        in_specs=[VM] * 3,
        out_specs=[VM] * 3,
        scratch_shapes=[pltpu.VMEM((16 * stride, 128), f32)],
        compiler_params=pltpu.CompilerParams(vmem_limit_bytes=8 << 20),
        cost_estimate=pl.CostEstimate(flops=10**9, bytes_accessed=10**6, transcendentals=0),
        name="core",
    )(block, band, bias)


def conv_kernel(block, core0, core1, core2, band, bias, out, buf0, buf1, mask):
    zh = lax.axis_index("frame") // 4
    row_mask(mask)
    src = block
    for layer, (dst, done) in enumerate(((buf0, core0), (buf1, core1), (buf0, core2))):
        width = done.shape[1]
        dst[stride * (5 + layer) : stride * (11 - layer), 0:width] = done[...]
        lines = [(1 + layer, 5 + layer), (11 - layer, 15 - layer)]
        for t in range(5 - layer):
            h = pair_rows(src, 0, lines, t, layer, band, bias)
            keep(h, dst, 0, lines, t, layer, mask)
        src = dst
    for t in range(2):
        h = pair_rows(src, 0, [(4, 12)], t, 3, band, bias)
        h = pltpu.roll(h, h.shape[0] - halo, 0)
        tiles = [h[stride * x : stride * x + 32] for x in range(8)]
        whole = jnp.concatenate(tiles, axis=0).T.astype(bf16)
        for i in range(2):
            out[(2 * t + i - zh) & 3] = whole[64 * i : 64 * i + 64]


def convolve(block, cores, band, bias):
    return pl.pallas_call(
        conv_kernel,
        out_shape=jax.ShapeDtypeStruct((4, 64, 256), bf16),
        in_specs=[VM] * 6,
        out_specs=VM,
        scratch_shapes=[
            pltpu.VMEM((16 * stride, 640), bf16),
            pltpu.VMEM((16 * stride, 512), bf16),
            pltpu.VMEM((16 * stride, 128), f32),
        ],
        compiler_params=pltpu.CompilerParams(vmem_limit_bytes=16 << 20),
        name="convolve",
    )(block, *cores, band, bias)


def place_kernel(own, high, far, low, out, rows):
    turn = 32 * (lax.axis_index("frame") % 4)
    parts = [r[...].astype(f32) for r in (own, high, far, low)]
    for x in range(8):
        line = jnp.concatenate([p[:, 32 * x : 32 * x + 32] for p in parts], axis=1)
        rows[pl.ds(x, 64, stride=8), :] = pltpu.roll(line, turn, 1)
    out[...] = rows[...].astype(bf16)


def place(own, high, far, low):
    return pl.pallas_call(
        place_kernel,
        out_shape=jax.ShapeDtypeStruct((512, 128), bf16),
        in_specs=[VM] * 4,
        out_specs=VM,
        scratch_shapes=[pltpu.VMEM((512, 128), f32)],
        compiler_params=pltpu.CompilerParams(vmem_limit_bytes=4 << 20),
        name="place",
    )(own, high, far, low)


def send(v, way, axis="frame"):
    return lax.ppermute(v, axis, way)


def only(inside, v):
    return jnp.where(inside, v, jnp.zeros_like(v))


def joined(features, voxel_embed, visible, w_query, w_key, w_value, w_out, conv_weight, conv_bias):
    around = range(4)
    x_by = lambda k: [(4 * z + x, 4 * z + (x + k) % 4) for z in around for x in around]
    up, down = x_by(1), x_by(3)
    z_up = [(i, (i + 4) % 16) for i in range(16)]
    z_down = [(j, i) for i, j in z_up]
    frames, planes, c = features.shape[:3]
    feat = features.reshape(frames, planes, c * 8, 128)
    embed = voxel_embed.reshape(planes, c * 8, 128)
    s2a, s2b, s1a, s1b = attend((2, 1), feat, embed, visible, w_query, w_key)
    from_low = send(s2a, up)
    from_high = send(s2b, down)
    s3a, s3b, s0a, s0b = attend((3, 0), feat, embed, visible, w_query, w_key)
    band, wide_v, wide_o = weights(conv_weight, w_value, w_out)
    high_a = send(s3a, down)
    low_a = send(merge([s1a, from_low], [8])[0], up)
    high_b = send(merge([s3b, from_high], [8])[0], down)
    low_b = send(s1b, up)
    z1, z2a, z2b = merge([s0a, low_a, high_a], [4, 2, 2])
    from_low = send(z2a, z_up)
    from_high = send(z2b, z_down)
    low = send(lift(0, z1, from_low), z_up)
    z3, z0 = merge([s0b, low_b, high_b], [4, 4])
    high = send(lift(2, z3, from_high), z_down)
    hidden = finish(z0, low, high, wide_v, wide_o).reshape(8, 32, 256)

    me = lax.axis_index("frame")
    zh, xi = me // 4, me % 4
    below = only(xi > 0, send(hidden, up))
    above = only(xi < 3, send(hidden, down))
    hidden = jnp.concatenate([below, hidden, above], axis=2)

    def where_is(x, chunk):
        return (4 * (chunk % 4) + x) * 4 + chunk // 4

    y_next = [(where_is(x, k), where_is(x, (k + 1) % 16)) for x in around for k in range(16)]
    y_prev = [(j, i) for i, j in y_next]
    chunk = lax.axis_index("by") * 4 + zh
    left = only(chunk > 0, send(hidden[:, -halo:], y_next, ("frame", "by")))
    right = only(chunk < 15, send(hidden[:, :halo], y_prev, ("frame", "by")))
    first, second = (
        jnp.concatenate([left[i], hidden[i], right[i]], axis=1)
        for i in (slice(0, halo), slice(halo, None))
    )
    x_next = [(i, (i + 1) % 4) for i in range(4)]
    x_prev = [(j, i) for i, j in x_next]
    bx = lax.axis_index("bx")
    front = only(bx > 0, send(second, x_next, "bx"))
    back = only(bx < 3, send(first, x_prev, "bx"))
    bias = jnp.concatenate([conv_bias, conv_bias], axis=1)

    def lines(*parts):
        whole = jnp.concatenate(parts, axis=0)
        pad = jnp.zeros((whole.shape[0], stride - 32 - 2 * halo, 768), bf16)
        return jnp.concatenate([whole, pad], axis=1).reshape(-1, 768)

    cores = core(lines(first, second), band, bias)
    out = convolve(lines(front, first, second, back), cores, band, bias)
    pieces = [
        send(out[r], [(4 * z + x, 4 * x + (z + r) % 4) for z in around for x in around])
        for r in around
    ]
    return place(pieces[0], pieces[3], pieces[2], pieces[1]).reshape(1, c, 8, 128)


def solution(mesh):
    return jax.shard_map(
        joined,
        mesh=mesh,
        in_specs=(
            P("frame", None, None, "bx", "by"),
            P(None, None, "bx", "by"),
            P("frame", None, "bx", "by"),
            P(),
            P(),
            P(),
            P(),
            P(),
            P(),
        ),
        out_specs=P("frame", None, "bx", "by"),
        check_vma=False,
    )
```

```python
import functools

import jax
import jax.numpy as jnp
from jax import lax
from jax.experimental import pallas as pl
from jax.experimental.pallas import tpu as pltpu
from jax.sharding import PartitionSpec as P


absent_score = -1e30
halo = 4
stride = 48
bf16, f32 = jnp.bfloat16, jnp.float32
VM = pl.BlockSpec(memory_space=pltpu.VMEM)


def dot(a, b):
    return jnp.dot(a, b, preferred_element_type=f32)


def lane_blocks(v):
    lane = lax.broadcasted_iota(jnp.int32, (8, 128), 1)
    low = lane < 64
    even = (lane & 63) < 32
    t = [None] * 4
    for i in (0, 1):
        t[i] = jnp.where(low, v[i], pltpu.roll(v[i + 2], 64, 1))
        t[i + 2] = jnp.where(low, pltpu.roll(v[i], 64, 1), v[i + 2])
    o = [None] * 4
    for i in (0, 2):
        o[i] = jnp.where(even, t[i], pltpu.roll(t[i + 1], 32, 1))
        o[i + 1] = jnp.where(even, pltpu.roll(t[i], 96, 1), t[i + 1])
    return o


def three_terms(m):
    hi = m.astype(bf16).astype(f32)
    mid = (m - hi).astype(bf16).astype(f32)
    return hi, mid, m - hi - mid


def attend_kernel(half, feat_at, embed_at, seen_at, wq_at, wk_at, *refs):
    outs, feat, embed, seen, wq, wk, key0, key1, wide0, wide1, sems = refs[:4], *refs[4:]
    steps, frames, n = feat.shape[:3]
    me = lax.axis_index("frame")
    zh, xi = me // 4, me % 4
    turn = (128 - 32 * xi) & 127

    def copies(s):
        block = 1 + 2 * half + s * n // 4
        z = pl.ds(((block + zh) & 3) * 4 + s * n % 4, n)
        return [
            pltpu.make_async_copy(embed_at.at[z], embed.at[s], sems.at[s, 0]),
            pltpu.make_async_copy(feat_at.at[:, z], feat.at[s], sems.at[s, 1]),
            pltpu.make_async_copy(seen_at.at[:, z], seen.at[s], sems.at[s, 2]),
        ]

    loads = [copies(s) for s in range(steps)]
    small = [
        pltpu.make_async_copy(wq_at, wq, sems.at[steps, 0]),
        pltpu.make_async_copy(wk_at, wk, sems.at[steps, 1]),
    ]
    for c in [loads[0][0], *small, *loads[0][1:], *sum(loads[1:], [])]:
        c.start()
    for c in small:
        c.wait()

    def keys(s):
        key = (key0, key1)[s % 2]
        loads[s][0].wait()
        for p in range(n):
            key[p] = embed[s, p].astype(f32)
        cols = [key[p, pl.ds(i, 64, stride=8), :] for p in range(n) for i in range(8)]
        wide = jnp.concatenate(cols, axis=1).astype(bf16)
        q = lax.dot_general(wq[...], wide, (((0,), (0,)), ((), ())), preferred_element_type=f32)
        qk = dot(wk[...], q.astype(bf16))
        for p in range(n):
            for i in range(8):
                at = (8 * p + i) * 128
                key[p, pl.ds(i, 64, stride=8), :] = qk[:, at : at + 128]

    def plane(s, p):
        key, wide = (key0, key1)[s % 2], (wide0, wide1)[p % 2]
        sums = [jnp.zeros((8, 128), f32) for _ in range(frames)]
        for g in range(16):
            rows = slice(32 * g, 32 * g + 32)
            line = key[p, rows, :]
            for f in range(frames):
                value = feat[s, f, p, rows, :].astype(f32)
                wide[f, rows, :] = value
                sums[f] = sums[f] + jnp.sum((line * value).reshape(4, 8, 128), axis=0)
        sums = [v * 0.125 for v in sums]
        ok = [seen[s, f, p] > 0 for f in range(frames)]
        m = jnp.full((8, 128), absent_score, f32)
        for f in range(frames):
            m = jnp.maximum(m, jnp.where(ok[f], sums[f], absent_score))
        e = [jnp.where(ok[f], jnp.exp(sums[f] - m), 0.0) for f in range(frames)]
        total = e[0]
        for f in range(1, frames):
            total = total + e[f]

        def put(g, tiles):
            tiles = [pltpu.roll(t, turn, 1) for t in tiles]
            for out, tile in zip(outs, lane_blocks(tiles)):
                out[s * n + p, 8 * g : 8 * g + 8, :] = tile.astype(bf16)

        for g in range(16):
            rows = slice(32 * g, 32 * g + 32)
            acc = None
            for f in range(frames):
                term = e[f][None] * wide[f, rows, :].reshape(4, 8, 128)
                acc = term if acc is None else acc + term
            put(g, [acc[i] for i in range(4)])
        put(16, [*three_terms(m), total])

    keys(0)
    for s in range(steps):
        loads[s][1].wait()
        loads[s][2].wait()
        if s + 1 < steps:
            keys(s + 1)
        for p in range(n):
            plane(s, p)


def attend(half, feat, embed, visible, w_query, w_key):
    frames, planes, rows = feat.shape[:3]
    c = w_key.shape[0]
    n = 2
    count = planes // 2
    steps = count // n
    hbm = pl.BlockSpec(memory_space=pltpu.HBM)
    return pl.pallas_call(
        functools.partial(attend_kernel, half),
        out_shape=[jax.ShapeDtypeStruct((count, 136, 128), bf16)] * 4,
        in_specs=[hbm] * 5,
        out_specs=[VM] * 4,
        scratch_shapes=[
            pltpu.VMEM((steps, frames, n, rows, 128), bf16),
            pltpu.VMEM((steps, n, rows, 128), bf16),
            pltpu.VMEM((steps, frames, n, 8, 128), jnp.int32),
            pltpu.VMEM((c, c), bf16),
            pltpu.VMEM((c, c), bf16),
            pltpu.VMEM((n, rows, 128), f32),
            pltpu.VMEM((n, rows, 128), f32),
            pltpu.VMEM((frames, rows, 128), f32),
            pltpu.VMEM((frames, rows, 128), f32),
            pltpu.SemaphoreType.DMA((steps + 1, 3)),
        ],
        compiler_params=pltpu.CompilerParams(vmem_limit_bytes=16 << 20),
        cost_estimate=pl.CostEstimate(flops=10**8, bytes_accessed=12 << 20, transcendentals=0),
        name="attend",
    )(*[pltpu.with_memory_space_constraint(v, pltpu.HBM) for v in (feat, embed, visible, w_query, w_key)])


def spread(v):
    u = v + pltpu.roll(v, 64, 1)
    return u + pltpu.roll(u, 32, 1)


def merged_plane(parts):
    lane = lax.broadcasted_iota(jnp.int32, (8, 128), 1)
    tail = lane >= 96
    stats = [r[p, 128:136, :].astype(f32) for r, p in parts]
    ms = [spread(jnp.where(tail, 0.0, s)) for s in stats]
    ls = [spread(jnp.where(tail, s, 0.0)) for s in stats]
    m = functools.reduce(jnp.maximum, ms)
    ws = [jnp.exp(v - m) for v in ms]
    total = sum(w * v for w, v in zip(ws, ls))
    return ws, total, m


def weighted_rows(parts, ws):
    acc = None
    for (r, p), w in zip(parts, ws):
        term = r[p, 0:128, :].astype(f32).reshape(16, 8, 128) * w[None]
        acc = term if acc is None else acc + term
    return acc.reshape(128, 128)


def merge_plane(out, i, parts):
    lane = lax.broadcasted_iota(jnp.int32, (8, 128), 1)
    ws, total, m = merged_plane(parts)
    out[i, 0:128, :] = weighted_rows(parts, ws).astype(bf16)
    hi, mid, low = three_terms(m)
    packed = jnp.where(
        lane < 32, hi, jnp.where(lane < 64, mid, jnp.where(lane >= 96, total, low))
    )
    out[i, 128:136, :] = packed.astype(bf16)


def merge_kernel(n, sizes, *refs):
    ins, outs = refs[:n], refs[n:]
    at = 0
    for out, size in zip(outs, sizes):
        for i in range(size):
            merge_plane(out, i, [(r, at) for r in ins])
            at += 1


def merge(parts, sizes):
    n = parts[0].shape[0]
    return pl.pallas_call(
        functools.partial(merge_kernel, len(parts), sizes),
        out_shape=[jax.ShapeDtypeStruct((s, 136, 128), bf16) for s in sizes],
        in_specs=[VM] * len(parts),
        out_specs=[VM] * len(sizes),
        compiler_params=pltpu.CompilerParams(vmem_limit_bytes=6 << 20),
        cost_estimate=pl.CostEstimate(flops=n * 10**5, bytes_accessed=n * 10**5, transcendentals=0),
        name="merge",
    )(*parts)


def lift_kernel(at, slot, came, out):
    other = 2 - at
    out[other : other + 2] = slot[other : other + 2]
    for i in range(2):
        merge_plane(out, at + i, [(slot, at + i), (came, i)])


def lift(at, slot, came):
    return pl.pallas_call(
        functools.partial(lift_kernel, at),
        out_shape=jax.ShapeDtypeStruct(slot.shape, bf16),
        in_specs=[VM] * 2,
        out_specs=VM,
        compiler_params=pltpu.CompilerParams(vmem_limit_bytes=4 << 20),
        cost_estimate=pl.CostEstimate(flops=10**5, bytes_accessed=10**5, transcendentals=0),
        name="lift",
    )(slot, came)


def finish_kernel(own, low, high, wv, wo, out, rows):
    for p in range(4):
        parts = [(own, p), (low, p), (high, p)]
        ws, total, _ = merged_plane(parts)
        inv = 1.0 / total
        rows[128 * p : 128 * p + 128, :] = weighted_rows(parts, [w * inv for w in ws])
    lines = []
    for x in range(8):
        t = rows[pl.ds(x, 64, stride=8), :].T
        lines.append(jnp.concatenate([t[32 * i : 32 * i + 32] for i in range(4)], axis=1))
    mixed = jnp.concatenate(lines, axis=0).astype(bf16)
    attended = dot(mixed, wv[...]).astype(bf16)
    out[...] = dot(attended, wo[...]).astype(bf16)


def finish(own, low, high, wv, wo):
    return pl.pallas_call(
        finish_kernel,
        out_shape=jax.ShapeDtypeStruct((256, 256), bf16),
        in_specs=[VM] * 5,
        out_specs=VM,
        scratch_shapes=[pltpu.VMEM((512, 128), f32)],
        compiler_params=pltpu.CompilerParams(vmem_limit_bytes=6 << 20),
        name="finish",
    )(own, low, high, wv, wo)


def weights_kernel(w, wv, wo, band, wide_v, wide_o, tmp):
    zero = jnp.zeros((64, 64), bf16)
    for tap in range(9):
        a = [w[0, 9 * i + tap] for i in range(3)]
        left = jnp.concatenate([a[0], a[1], a[2], zero], axis=0)
        right = jnp.concatenate([zero, a[0], a[1], a[2]], axis=0)
        e = tap % 3
        band[0, tap // 3, :, 128 * e : 128 * e + 128] = jnp.concatenate([left, right], axis=1)

    @pl.when(pl.program_id(0) == 0)
    def _():
        tmp[...] = wv[...].astype(f32)
        blank = jnp.zeros((16, 64), f32)
        for i in range(4):
            piece = tmp[pl.ds(i, 16, stride=4), :]
            for p in range(4):
                line = jnp.concatenate([piece if j == p else blank for j in range(4)], axis=1)
                at = 64 * i + 16 * p
                wide_v[at : at + 16, :] = line.astype(bf16)
        for p in range(4):
            line = jnp.concatenate([wo[...] if j == p else zero for j in range(4)], axis=1)
            wide_o[64 * p : 64 * p + 64, :] = line


def weights(conv_weight, w_value, w_out):
    layers = conv_weight.shape[0]
    small = pl.BlockSpec((64, 64), lambda i: (0, 0))
    big = pl.BlockSpec((256, 256), lambda i: (0, 0))
    return pl.pallas_call(
        weights_kernel,
        out_shape=[
            jax.ShapeDtypeStruct((layers, 3, 256, 384), bf16),
            jax.ShapeDtypeStruct((256, 256), bf16),
            jax.ShapeDtypeStruct((256, 256), bf16),
        ],
        grid=(layers,),
        in_specs=[pl.BlockSpec((1, 27, 64, 64), lambda i: (i, 0, 0, 0)), small, small],
        out_specs=[pl.BlockSpec((1, 3, 256, 384), lambda i: (i, 0, 0, 0)), big, big],
        scratch_shapes=[pltpu.VMEM((64, 64), f32)],
        compiler_params=pltpu.CompilerParams(
            dimension_semantics=("arbitrary",), vmem_limit_bytes=8 << 20
        ),
        cost_estimate=pl.CostEstimate(flops=10**6, bytes_accessed=8 << 20, transcendentals=0),
        name="weights",
    )(conv_weight.reshape(layers, 27, 64, 64), w_value, w_out)


def row_mask(mask):
    xi = lax.axis_index("frame") % 4
    x0, y0 = lax.axis_index("bx") * 8 - halo, lax.axis_index("by") * 128 + xi * 32 - halo
    y = lax.broadcasted_iota(jnp.int32, (stride, 128), 0) + y0
    y_ok = (y >= 0) & (y < 512)
    for x in range(16):
        line = jnp.where(y_ok & (x0 + x >= 0) & (x0 + x < 32), 1.0, 0.0)
        mask[stride * x : stride * x + stride, :] = line


def pair_rows(src, shift, lines, t, layer, band, bias):
    acc = None
    for b in range(3):
        at = [(stride * (i - shift + b - 1), stride * (j - shift + b - 1)) for i, j in lines]
        rows = [src[i:j, 128 * t : 128 * t + 256] for i, j in at]
        rows = rows[0] if len(rows) == 1 else jnp.concatenate(rows, axis=0)
        term = dot(rows, band[layer, b])
        acc = term if acc is None else acc + term
    n = acc.shape[0]
    h = acc[:, 128:256] + bias[layer : layer + 1, :]
    return h + pltpu.roll(acc[:, 0:128], 1, 0) + pltpu.roll(acc[:, 256:384], n - 1, 0)


def keep(h, dst, shift, lines, t, layer, mask):
    z0 = lax.axis_index("frame") // 4 * 4 - halo
    lane = lax.broadcasted_iota(jnp.int32, (1, 128), 1)
    z = z0 + layer + 1 + 2 * t + lane // 64
    z_ok = jnp.where((z >= 0) & (z < 16), 1.0, 0.0)
    at = 0
    for i, j in lines:
        n = stride * (j - i)
        ok = z_ok * mask[stride * i : stride * j, :]
        part = jnp.where(ok > 0, jnp.maximum(h[at : at + n], 0.0), 0.0)
        row = stride * (i - shift)
        dst[row : row + n, 128 * t : 128 * t + 128] = part.astype(bf16)
        at += n


def core_kernel(block, band, bias, out0, out1, out2, mask):
    row_mask(mask)
    src, shift = block, 4
    for layer, dst in enumerate((out0, out1, out2)):
        lines = [(5 + layer, 11 - layer)]
        for t in range(5 - layer):
            h = pair_rows(src, shift, lines, t, layer, band, bias)
            keep(h, dst, 5 + layer, lines, t, layer, mask)
        src, shift = dst, 5 + layer


def core(block, band, bias):
    widths = (640, 512, 384)
    return pl.pallas_call(
        core_kernel,
        out_shape=[
            jax.ShapeDtypeStruct((stride * (6 - 2 * i), w), bf16) for i, w in enumerate(widths)
        ],
        in_specs=[VM] * 3,
        out_specs=[VM] * 3,
        scratch_shapes=[pltpu.VMEM((16 * stride, 128), f32)],
        compiler_params=pltpu.CompilerParams(vmem_limit_bytes=8 << 20),
        cost_estimate=pl.CostEstimate(flops=10**9, bytes_accessed=10**6, transcendentals=0),
        name="core",
    )(block, band, bias)


def conv_kernel(block, core0, core1, core2, band, bias, out, buf0, buf1, mask):
    xi = lax.axis_index("frame") % 4
    row_mask(mask)
    src = block
    for layer, (dst, done) in enumerate(((buf0, core0), (buf1, core1), (buf0, core2))):
        width = done.shape[1]
        dst[stride * (5 + layer) : stride * (11 - layer), 0:width] = done[...]
        lines = [(1 + layer, 5 + layer), (11 - layer, 15 - layer)]
        for t in range(5 - layer):
            h = pair_rows(src, 0, lines, t, layer, band, bias)
            keep(h, dst, 0, lines, t, layer, mask)
        src = dst
    for t in range(2):
        h = pair_rows(src, 0, [(4, 12)], t, 3, band, bias)
        h = pltpu.roll(h, h.shape[0] - halo, 0)
        tiles = [h[stride * x : stride * x + 32] for x in range(8)]
        whole = jnp.concatenate(tiles, axis=0).T.astype(bf16)
        for i in range(2):
            out[(2 * t + i - xi) & 3] = whole[64 * i : 64 * i + 64]


def convolve(block, cores, band, bias):
    return pl.pallas_call(
        conv_kernel,
        out_shape=jax.ShapeDtypeStruct((4, 64, 256), bf16),
        in_specs=[VM] * 6,
        out_specs=VM,
        scratch_shapes=[
            pltpu.VMEM((16 * stride, 640), bf16),
            pltpu.VMEM((16 * stride, 512), bf16),
            pltpu.VMEM((16 * stride, 128), f32),
        ],
        compiler_params=pltpu.CompilerParams(vmem_limit_bytes=16 << 20),
        name="convolve",
    )(block, *cores, band, bias)


def place_kernel(own, high, far, low, out, rows):
    turn = 32 * (lax.axis_index("frame") % 4)
    parts = [r[...].astype(f32) for r in (own, high, far, low)]
    for x in range(8):
        line = jnp.concatenate([p[:, 32 * x : 32 * x + 32] for p in parts], axis=1)
        rows[pl.ds(x, 64, stride=8), :] = pltpu.roll(line, turn, 1)
    out[...] = rows[...].astype(bf16)


def place(own, high, far, low):
    return pl.pallas_call(
        place_kernel,
        out_shape=jax.ShapeDtypeStruct((512, 128), bf16),
        in_specs=[VM] * 4,
        out_specs=VM,
        scratch_shapes=[pltpu.VMEM((512, 128), f32)],
        compiler_params=pltpu.CompilerParams(vmem_limit_bytes=4 << 20),
        name="place",
    )(own, high, far, low)


def send(v, way, axis="frame"):
    return lax.ppermute(v, axis, way)


def only(inside, v):
    return jnp.where(inside, v, jnp.zeros_like(v))


def sides(place, from_even, from_odd):
    is_odd = place % 2 == 1
    before = jnp.where(is_odd, from_even, from_odd)
    after = jnp.where(is_odd, from_odd, from_even)
    return only(place > 0, before), only(place < 3, after)


def joined(features, voxel_embed, visible, w_query, w_key, w_value, w_out, conv_weight, conv_bias):
    around = range(4)
    x_by = lambda k: [(4 * z + x, 4 * z + (x + k) % 4) for z in around for x in around]
    up, down = x_by(1), x_by(3)
    z_up = [(i, (i + 4) % 16) for i in range(16)]
    z_down = [(j, i) for i, j in z_up]
    frames, planes, c = features.shape[:3]
    feat = features.reshape(frames, planes, c * 8, 128)
    embed = voxel_embed.reshape(planes, c * 8, 128)
    a0, a1, a2, a3 = attend(0, feat, embed, visible, w_query, w_key)
    from_low = send(a2, up)
    high_a = send(a3, down)
    b0, b1, b2, b3 = attend(1, feat, embed, visible, w_query, w_key)
    band, wide_v, wide_o = weights(conv_weight, w_value, w_out)
    from_high = send(b2, down)
    low_b = send(b1, up)
    low_a = send(merge([a1, from_low], [8])[0], up)
    high_b = send(merge([b3, from_high], [8])[0], down)
    z1, z2a, z2b = merge([a0, low_a, high_a], [4, 2, 2])
    from_low = send(z2a, z_up)
    from_high = send(z2b, z_down)
    low = send(lift(0, z1, from_low), z_up)
    z3, z0 = merge([b0, low_b, high_b], [4, 4])
    high = send(lift(2, z3, from_high), z_down)
    hidden = finish(z0, low, high, wide_v, wide_o).reshape(8, 32, 256)

    even = {i: i ^ 1 for i in range(4)}
    odd = {0: 0, 1: 2, 2: 1, 3: 3}
    me = lax.axis_index("frame")
    zh, xi = me // 4, me % 4
    z_pairs = [[(4 * z + x, 4 * p[z] + x) for z in around for x in around] for p in (even, odd)]
    below, above = sides(zh, send(hidden, z_pairs[0]), send(hidden, z_pairs[1]))
    hidden = jnp.concatenate([below, hidden, above], axis=2)

    def where_is(z, chunk):
        return (4 * z + chunk % 4) * 4 + chunk // 4

    y_next = [(where_is(z, k), where_is(z, (k + 1) % 16)) for z in range(4) for k in range(16)]
    y_prev = [(j, i) for i, j in y_next]
    chunk = lax.axis_index("by") * 4 + xi
    left = only(chunk > 0, send(hidden[:, -halo:], y_next, ("frame", "by")))
    right = only(chunk < 15, send(hidden[:, :halo], y_prev, ("frame", "by")))
    first, second = (
        jnp.concatenate([left[i], hidden[i], right[i]], axis=1)
        for i in (slice(0, halo), slice(halo, None))
    )
    bx = lax.axis_index("bx")
    is_odd = bx % 2 == 1
    front, back = sides(
        bx,
        send(jnp.where(is_odd, first, second), list(even.items()), "bx"),
        send(jnp.where(is_odd, second, first), list(odd.items()), "bx"),
    )
    bias = jnp.concatenate([conv_bias, conv_bias], axis=1)

    def lines(*parts):
        whole = jnp.concatenate(parts, axis=0)
        pad = jnp.zeros((whole.shape[0], stride - 32 - 2 * halo, 768), bf16)
        return jnp.concatenate([whole, pad], axis=1).reshape(-1, 768)

    cores = core(lines(first, second), band, bias)
    out = convolve(lines(front, first, second, back), cores, band, bias)
    low = send(out[1], up)
    high = send(out[3], down)
    far = send(out[2], x_by(2))
    return place(out[0], high, far, low).reshape(1, c, 8, 128)


def solution(mesh):
    return jax.shard_map(
        joined,
        mesh=mesh,
        in_specs=(
            P("frame", None, None, "bx", "by"),
            P(None, None, "bx", "by"),
            P("frame", None, "bx", "by"),
            P(),
            P(),
            P(),
            P(),
            P(),
            P(),
        ),
        out_specs=P("frame", None, "bx", "by"),
        check_vma=False,
    )
```
